512 devices in a mesh: patch: 64 (over z, y_lo, core), band: 8 (over x, y_hi).
Axes of the slice: x: 4, y: 4 (y_hi: 2, y_lo: 2; y = y_hi * 2 + y_lo), z: 16, core: 2. Of those that a mesh axis runs over, the one named last changes fastest.
Arguments:
- tile_flux: bfloat16 [6, 8192, 8, 128], P(None, ('patch', 'band')), may hold values from -6 to 6
- tile_weight: bfloat16 [6, 8192, 8, 128], P(None, ('patch', 'band')), may hold values from 0.19921875 to 5
- dest_patch: int32 [6, 8192], P(None, ('patch', 'band')), may hold values from 0 to 63, as said below
- dest_block: int32 [6, 8192], P(None, ('patch', 'band')), may hold values from 0 to 15, as said below
- basis: bfloat16 [2, 21, 31], replicated, may hold values from -1 to 1
- spatial: float32 [64, 6, 3, 21], P('patch'), may hold values from -1.25 to 1.25
Outputs:
- coadd: float32 [64, 256, 512], P('patch', 'band')
The draws below stay inside these ranges and needn't reach their ends.
Inputs may be any that keep to these rules, and one draw needn't show every extreme that they name: `dest_patch`: for each visit, the tiles held by one device go to exactly 8 different patches, 2 tiles to each. `dest_block`: for each visit, every block of every band of every patch receives exactly one tile.
All inputs are finite; a program needn't handle non-finite values.
Results may differ from the reference program's by a relative error of at most 0.0029.
Values may be sent and summed in bfloat16 or wider, within the bound.
A program may use at most 64 MiB of HBM per device.

```python
import math
import jax
import jax.numpy as jnp
from jax import lax

BASIS = 21
TAPS = 31
VISITS = 6
ROWS = 32
COLS = 512
TILE_ROWS = 8
TILE_COLS = 128
CAP = 2
TILES_V = 16
PATCHES = 64
TILES_ALL = 8192
PATCH_ROWS = 256
N_BAND = 8


def shuffled_patches(key):
    count = TILES_V // CAP
    scores = jax.random.permutation(jax.random.fold_in(key, 1), PATCHES).astype(jnp.int32)
    ids = jnp.arange(PATCHES, dtype=jnp.int32)
    scores = jnp.where(ids == 1, -1, scores)
    scores = jnp.where(ids == PATCHES // 2, -2, scores)
    chosen = jnp.argsort(scores, stable=True)[:count].astype(jnp.int32)
    order = jax.random.permutation(jax.random.fold_in(key, 2), count)
    return chosen[order]


def shuffled_blocks(key):
    return jax.random.permutation(key, TILES_V)


def routing_tables(key):
    count = TILES_V // CAP
    shift_keys = jax.random.split(jax.random.fold_in(key, 101), VISITS)
    order_keys = jax.random.split(jax.random.fold_in(key, 202), VISITS)
    shifts = jax.vmap(shuffled_patches)(shift_keys)
    orders = jax.vmap(shuffled_blocks)(order_keys)
    offsets = jax.random.randint(jax.random.fold_in(key, 303), (VISITS, PATCHES), 0, count)
    tile_ids = jnp.arange(TILES_ALL, dtype=jnp.int32)
    source = tile_ids // (N_BAND * TILES_V)
    within = tile_ids % TILES_V
    target = (source[None, :] + shifts[:, within // CAP]) % PATCHES
    lifted = jnp.take_along_axis(offsets, target, axis=1)
    block = jnp.take_along_axis(orders, (within[None, :] + CAP * lifted) % TILES_V, axis=1)
    return (target.astype(jnp.int32), block.astype(jnp.int32))


def draw_dest_patch(key, part):
    return routing_tables(key)[0]


def draw_dest_block(key, part):
    return routing_tables(key)[1]


def shard_levels(stream_key, extent, cuts, low, top_value):
    def one(position, parts):
        draws = jax.random.uniform(jax.random.fold_in(jax.random.fold_in(stream_key, 6), position), (parts,), jnp.float32, low / len(cuts), top_value / len(cuts))
        return jnp.repeat(jnp.exp(draws), extent[position] // parts).reshape((-1,) + (1,) * (len(extent) - position - 1))

    level = one(*cuts[0])
    for cut in cuts[1:]:
        level = level * one(*cut)
    return level


def bell_draw(key, shape, scale, bound, cuts=(), kind=jnp.bfloat16):
    values = scale * jax.random.normal(key, shape, jnp.float32)
    if cuts:
        values = values * shard_levels(key, shape, cuts, -0.22, 0.18)
    return jnp.clip(values, -bound, bound).astype(kind)


def setup_inputs(seed: int = 0) -> dict:
    splits = jax.random.split(jax.random.key(seed), 7)
    return {
        "tile_flux": bell_draw(splits[0], (VISITS, TILES_ALL, TILE_ROWS, TILE_COLS), 1.0, 6.0, ((1, 512),)),
        "tile_weight": jnp.clip(jnp.exp(math.log(5.0) - 3.2227897 * jax.random.uniform(splits[1], (VISITS, TILES_ALL, TILE_ROWS, TILE_COLS), jnp.float32) ** shard_levels(splits[1], (VISITS, TILES_ALL, TILE_ROWS, TILE_COLS), ((1, 512),), -0.2, 0.2)), 0.19921875, 5.0).astype(jnp.bfloat16),
        "dest_patch": draw_dest_patch(jax.random.fold_in(splits[6], 71), 0),
        "dest_block": draw_dest_block(jax.random.fold_in(splits[6], 71), 0),
        "basis": bell_draw(splits[4], (2, BASIS, TAPS), TAPS ** -0.5, 1.0),
        "spatial": bell_draw(splits[5], (PATCHES, VISITS, 3, BASIS), BASIS ** -0.5, 1.25, ((0, 64),), jnp.float32),
    }


def column_table(basis):
    width = 128 + TAPS - 1
    inner = jnp.arange(width)[:, None, None]
    outer = jnp.arange(128)[None, :, None]
    offset = jnp.arange(TAPS)[None, None, :]
    ones = (inner - outer == offset).astype(jnp.float32)
    table = jnp.einsum("iot,bt->ibo", ones, basis[0].astype(jnp.float32))
    return table.reshape(width, BASIS * 128).astype(jnp.bfloat16)


def row_table(basis):
    target = jnp.arange(ROWS)[:, None, None]
    source = jnp.arange(ROWS + TAPS - 1)[None, :, None]
    offset = jnp.arange(TAPS)[None, None, :]
    ones = (source - target == offset).astype(jnp.float32)
    table = jnp.einsum("stk,bk->bst", ones, basis[1].astype(jnp.float32))
    return table.astype(jnp.bfloat16)


def column_filter(rows_block, table):
    margin = TAPS // 2
    padded = jnp.pad(rows_block, ((0, 0), (margin, margin)))
    pieces = jnp.stack([padded[:, 128 * column:128 * column + 128 + TAPS - 1] for column in range(COLS // 128)], axis=1)
    result = jnp.dot(pieces.reshape(-1, 128 + TAPS - 1), table, preferred_element_type=jnp.float32)
    return result.astype(jnp.bfloat16).reshape(rows_block.shape[0], COLS // 128, BASIS, 128)


def reference(tile_flux, tile_weight, dest_patch, dest_block, basis, spatial):
    blocks_across = COLS // TILE_COLS
    margin = TAPS // 2
    tile_ids = jnp.arange(TILES_ALL, dtype=jnp.int32)
    band_of = (tile_ids // TILES_V) % N_BAND
    row_block = dest_block // blocks_across
    col_block = dest_block % blocks_across
    visit_ids = jnp.broadcast_to(jnp.arange(VISITS, dtype=jnp.int32)[:, None], dest_patch.shape)
    band_ids = jnp.broadcast_to(band_of[None, :], dest_patch.shape)
    shape = (VISITS, PATCHES, N_BAND, ROWS // TILE_ROWS, blocks_across, TILE_ROWS, TILE_COLS)
    grid = jnp.zeros(shape, jnp.bfloat16).at[visit_ids, dest_patch, band_ids, row_block, col_block].set(tile_flux)
    frames = grid.transpose(0, 1, 2, 3, 5, 4, 6).reshape(VISITS, PATCHES, PATCH_ROWS, COLS)
    wgrid = jnp.zeros(shape, jnp.float32).at[visit_ids, dest_patch, band_ids, row_block, col_block].set(tile_weight.astype(jnp.float32))
    weight_map = wgrid.transpose(0, 1, 2, 3, 5, 4, 6).reshape(VISITS, PATCHES, PATCH_ROWS, COLS)
    ctable = column_table(basis)
    rtable = row_table(basis).astype(jnp.float32)
    col_coord = ((2.0 * jnp.arange(COLS, dtype=jnp.float32) + 1.0) / COLS - 1.0).reshape(COLS // 128, 128)

    def one_patch(inputs):
        frames_q, weights_q, spatial_q = inputs
        padded = jnp.pad(frames_q, ((0, 0), (margin, margin), (0, 0)))
        filtered = column_filter(padded.reshape(-1, COLS), ctable)
        filtered = filtered.reshape(VISITS, PATCH_ROWS + 2 * margin, COLS // 128, BASIS, 128)
        pieces = []
        for band in range(N_BAND):
            part = filtered[:, band * ROWS:band * ROWS + ROWS + 2 * margin].astype(jnp.float32)
            smoothed = jnp.einsum("bst,vtcbo->vscbo", rtable, part)
            mixture = jnp.einsum("vscbo,vjb->vjsco", smoothed, spatial_q, precision=lax.Precision.HIGHEST)
            row_coord = (2.0 * (band * ROWS + jnp.arange(ROWS, dtype=jnp.float32)) + 1.0) / PATCH_ROWS - 1.0
            matched = mixture[:, 0] + row_coord[None, :, None, None] * mixture[:, 1] + col_coord[None, None] * mixture[:, 2]
            pieces.append(matched.reshape(VISITS, ROWS, COLS))
        matched = jnp.concatenate(pieces, axis=1)
        return jnp.sum(weights_q * matched, axis=0) / jnp.sum(weights_q, axis=0)

    return lax.map(one_patch, (frames.transpose(1, 0, 2, 3), weight_map.transpose(1, 0, 2, 3), spatial))
```

```python
import jax
import jax.numpy as jnp
import numpy as np
from jax import lax
from jax.experimental import pallas as pl
from jax.experimental.pallas import tpu as pltpu
from jax.sharding import PartitionSpec as P

MESH = pl.DeviceIdType.MESH
VISITS = 6
BASIS = 21
TAPS = 31
ROWS = 32
COLS = 512
ROUNDS = 3
PAIRS = (BASIS + 1) // 2
DEPTH = PAIRS * 128


def exchange_kernel(t_ref, k_ref, g_ref, h_ref, y, keys, z, s1, s1b, r1, sk, rk, s2, r2, sh, rh):
    n, bands = lax.axis_size("patch"), lax.axis_size("band")
    me, band = lax.axis_index("patch"), lax.axis_index("band")
    chips = n // 2
    chip, core = me // 2, me % 2

    barrier = pltpu.get_barrier_semaphore()

    def greet(d, carry):
        pl.semaphore_signal(
            barrier, inc=1, device_id={"patch": (me + d) % n}, device_id_type=MESH
        )
        return carry

    lax.fori_loop(1, n, greet, 0)

    @pl.when(band > 0)
    def _():
        pl.semaphore_signal(barrier, inc=1, device_id={"band": band - 1}, device_id_type=MESH)

    @pl.when(band < bands - 1)
    def _():
        pl.semaphore_signal(barrier, inc=1, device_id={"band": band + 1}, device_id_type=MESH)

    pl.semaphore_wait(
        barrier, n - 1 + (band + bands - 1) // bands + (2 * bands - 2 - band) // bands
    )

    def partner(i, count):
        half = (i + 1) // 2
        return count // 2 + half * (1 - 2 * (i % 2))

    def send_keys(i, carry):
        peer = (me + partner(i, n)) % n
        pltpu.make_async_remote_copy(
            k_ref.at[0], keys.at[me], sk, rk, device_id={"patch": peer}, device_id_type=MESH
        ).start()
        return carry

    lax.fori_loop(0, n - 1, send_keys, 0)
    pltpu.make_async_copy(k_ref.at[0], keys.at[me], rk).start()

    for q in range(ROUNDS):
        owner = q % 2

        def send_rows(i, carry):
            c = (chip + partner(i, chips)) % chips
            pltpu.make_async_remote_copy(
                t_ref.at[q * chips + c],
                y.at[q, me],
                s1.at[q],
                r1.at[q],
                device_id={"patch": 2 * c + owner},
                device_id_type=MESH,
            ).start()
            return carry

        lax.fori_loop(0, chips - 1, send_rows, 0)

        @pl.when(core == owner)
        def _():
            pltpu.make_async_copy(t_ref.at[q * chips + chip], y.at[q, me], r1.at[q]).start()

        @pl.when(core != owner)
        def _():
            pltpu.make_async_remote_copy(
                t_ref.at[q * chips + chip],
                y.at[q, me],
                s1b.at[q],
                r1.at[q],
                device_id={"patch": 2 * chip + owner},
                device_id_type=MESH,
            ).start()

    pltpu.make_async_copy(keys, keys, rk).wait()

    def relay(q):
        group = lax.broadcasted_iota(jnp.int32, (64, 128), 0) % 8
        lane_slot = lax.broadcasted_iota(jnp.int32, (64, 128), 1) // 16
        table = keys[:, 0, :]
        rows = []
        for visit in (2 * q, 2 * q + 1):
            picked = jnp.where((group + visit) % 8 == lane_slot, table, 0)
            picked = jnp.sum(picked.reshape(8, 8, 128), axis=1)
            rows.append(pltpu.roll(picked, (128 - 16 * visit) % 128, 1))
        second = jnp.broadcast_to(chip // (chips // 2), (8, 128))
        wanted = jnp.where(second == 0, rows[0], rows[1])
        pltpu.make_async_copy(y.at[q], y.at[q], r1.at[q]).wait()
        data = y[q].reshape(n * 16, 128)
        for part in range(4):
            place = lax.broadcasted_iota(jnp.int32, (256, 128), 0) + 256 * part
            chosen = jnp.concatenate(
                [
                    jnp.where(
                        jnp.broadcast_to(wanted[g : g + 1], (256, 128)) == place, 1.0, 0.0
                    ).astype(jnp.bfloat16)
                    for g in range(8)
                ],
                axis=1,
            )
            moved = jnp.dot(chosen, data, preferred_element_type=jnp.float32)
            z[q, part * 16 : (part + 1) * 16] = moved.reshape(16, 2, 8, 128).astype(jnp.bfloat16)

        def send_blocks(i, carry):
            peer = (me + partner(i, n)) % n
            pltpu.make_async_remote_copy(
                z.at[q, peer],
                g_ref.at[q * chips + chip],
                s2.at[q],
                r2.at[q],
                device_id={"patch": peer},
                device_id_type=MESH,
            ).start()
            return carry

        lax.fori_loop(0, n - 1, send_blocks, 0)
        pltpu.make_async_copy(z.at[q, me], g_ref.at[q * chips + chip], r2.at[q]).start()

    @pl.when(core == 0)
    def _():
        relay(0)
        relay(2)

    @pl.when(core == 1)
    def _():
        relay(1)

    def halo(visit, side):
        half, step = (1, 1) if side == 0 else (0, -1)
        return pltpu.make_async_remote_copy(
            g_ref.at[pl.ds(visit * 16, 8), half],
            h_ref.at[visit, side],
            sh.at[visit, side],
            rh.at[visit, side],
            device_id={"band": band + step},
            device_id_type=MESH,
        )

    for q in range(ROUNDS):
        part = g_ref.at[pl.ds(q * chips, chips)]
        pltpu.make_async_copy(part, part, r2.at[q]).wait()

        @pl.when(band < bands - 1)
        def _():
            halo(2 * q, 0).start()
            halo(2 * q + 1, 0).start()

        @pl.when(band > 0)
        def _():
            halo(2 * q, 1).start()
            halo(2 * q + 1, 1).start()

    @pl.when(band < bands - 1)
    def _():
        for visit in range(VISITS):
            halo(visit, 0).wait_send()
            halo(visit, 1).wait_recv()

    @pl.when(band > 0)
    def _():
        for visit in range(VISITS):
            halo(visit, 1).wait_send()
            halo(visit, 0).wait_recv()

    pltpu.make_async_copy(keys.at[pl.ds(0, n - 1)], keys.at[pl.ds(0, n - 1)], sk).wait()
    for q in range(ROUNDS):
        owner = q % 2
        sent = t_ref.at[pl.ds(0, chips - 1)]
        pltpu.make_async_copy(sent, sent, s1.at[q]).wait()

        @pl.when(core != owner)
        def _():
            pltpu.make_async_copy(t_ref.at[0], t_ref.at[0], s1b.at[q]).wait()

        @pl.when(core == owner)
        def _():
            relayed = z.at[q, pl.ds(0, n - 1)]
            pltpu.make_async_copy(relayed, relayed, s2.at[q]).wait()


def coadd_kernel(g_ref, h_ref, order_ref, worder_ref, cbase_ref, rbase_ref, coef_ref, o_ref,
                 ctable, rtable, filtered, num, den):
    band, bands = lax.axis_index("band"), lax.axis_size("band")
    row = lax.broadcasted_iota(jnp.int32, (128, 128), 0)
    lane = lax.broadcasted_iota(jnp.int32, (128, 128), 1)
    near = jnp.abs(row - lane) <= TAPS // 2
    for b in range(BASIS):
        taps = jnp.broadcast_to(cbase_ref[b : b + 1, :], (128, 128))
        cyclic = pltpu.roll(taps, 0, 1, stride=1, stride_axis=0)
        span = slice(b * 128, (b + 1) * 128)
        ctable[0:128, span] = jnp.where(near, cyclic, 0.0).astype(jnp.bfloat16)
        ctable[128:256, span] = jnp.where(near, 0.0, cyclic).astype(jnp.bfloat16)
    for pair in range(PAIRS):
        taps = jnp.broadcast_to(rbase_ref[pair : pair + 1, :], (ROWS, 128))
        rtable[:, pair * 128 : (pair + 1) * 128] = pltpu.roll(taps, 0, 1, stride=1, stride_axis=0)
    filtered[BASIS * 64 :, :] = jnp.zeros((DEPTH - BASIS * 64, COLS), jnp.bfloat16)
    num[...] = jnp.zeros_like(num)
    den[...] = jnp.zeros_like(den)
    first = (band * ROWS).astype(jnp.float32)
    rows_in = lax.broadcasted_iota(jnp.int32, (ROWS, 1), 0).astype(jnp.float32) + first
    u = (2.0 * rows_in + 1.0) / (bands * ROWS) - 1.0
    cols_in = lax.broadcasted_iota(jnp.int32, (1, COLS), 1).astype(jnp.float32)
    w = (2.0 * cols_in + 1.0) / COLS - 1.0
    above_on = jnp.broadcast_to(band, (8, 128)) > 0
    below_on = jnp.broadcast_to(band, (8, 128)) < bands - 1
    left_lane = lax.broadcasted_iota(jnp.int32, (256, 128), 1) < 64

    def one_visit(visit, carry):
        unit = visit * 16
        above = [jnp.where(above_on, h_ref[visit, 0, r].astype(jnp.float32), 0.0) for r in range(8)]
        below = [jnp.where(below_on, h_ref[visit, 1, r].astype(jnp.float32), 0.0) for r in range(8)]
        inner = [g_ref[unit + r, half].astype(jnp.float32) for r in range(8) for half in range(2)]
        rows = jnp.concatenate(above + inner + below, axis=0).astype(jnp.bfloat16)
        moved = jnp.dot(order_ref[...], rows, preferred_element_type=jnp.float32)
        beside = jnp.where(left_lane, moved[256:512], moved[512:768])
        window = jnp.concatenate([moved[0:256], beside], axis=1).astype(jnp.bfloat16)
        for b in range(BASIS):
            result = jnp.dot(
                window, ctable[:, b * 128 : (b + 1) * 128], preferred_element_type=jnp.float32
            ).astype(jnp.bfloat16)
            for c in range(4):
                filtered[b * 64 : (b + 1) * 64, c * 128 : (c + 1) * 128] = result[
                    c * 64 : (c + 1) * 64
                ]
        coef = coef_ref[visit]
        table = rtable[...]
        steady = table * (coef[0:1] + u * coef[1:2])
        slope = table * coef[2:3]
        exact = jnp.concatenate([steady, slope], axis=0)
        high = exact.astype(jnp.bfloat16)
        low = (exact - high.astype(jnp.float32)).astype(jnp.bfloat16)
        mixed = jnp.dot(
            jnp.concatenate([high, low], axis=0), filtered[...], preferred_element_type=jnp.float32
        )
        mixed = mixed[0:64] + mixed[64:128]
        matched = mixed[0:ROWS] + w * mixed[ROWS:64]
        weights = [g_ref[unit + 8 + r, half].astype(jnp.float32) for r in range(8) for half in range(2)]
        weights = jnp.concatenate(weights, axis=0).astype(jnp.bfloat16)
        weights = jnp.dot(worder_ref[...], weights, preferred_element_type=jnp.float32)
        weights = jnp.concatenate([weights[c * ROWS : (c + 1) * ROWS] for c in range(4)], axis=1)
        num[...] += weights * matched
        den[...] += weights
        return carry

    lax.fori_loop(0, VISITS, one_visit, 0)
    o_ref[...] = num[...] / den[...]


def orders():
    order = np.zeros((3, 4, 64, 256), np.float32)
    for c in range(4):
        for t in range(64):
            for kind, shift in ((0, 0), (1, 1), (2, -1)):
                d = c + shift
                if not 0 <= d < 4:
                    continue
                if t < 16:
                    place = (t % 8) * 8 + (t // 8) * 4 + d
                elif t < 48:
                    s = t - 16
                    place = 64 + (s % 8) * 16 + (s // 8) * 4 + d
                else:
                    s = t - 48
                    place = 192 + (s % 8) * 8 + (s // 8) * 4 + d
                order[kind, c, t, place] = 1.0
    worder = np.zeros((4, ROWS, 128), np.float32)
    for c in range(4):
        for s in range(ROWS):
            worder[c, s, (s % 8) * 16 + (s // 8) * 4 + c] = 1.0
    return order.reshape(768, 256), worder.reshape(128, 128)


def per_device(tile_flux, tile_weight, dest_patch, dest_block, basis, spatial):
    n = lax.axis_size("patch")
    chips = n // 2
    me = lax.axis_index("patch")
    units = jnp.stack([tile_flux, tile_weight], axis=1).transpose(0, 1, 3, 2, 4)
    units = units.reshape(VISITS * 16, 16, 128)
    key = dest_patch * 16 + dest_block
    slot = (jnp.arange(VISITS)[None, :, None] + me) % 8 == jnp.arange(8)[:, None, None]
    key_row = jnp.sum(jnp.where(slot, key[None], 0), axis=1).reshape(1, 1, 128)

    vmem = pl.BlockSpec(memory_space=pltpu.VMEM)
    dma = pltpu.SemaphoreType.DMA
    received, halo = pl.pallas_call(
        exchange_kernel,
        out_shape=(
            jax.ShapeDtypeStruct((VISITS * 16, 2, 8, 128), jnp.bfloat16),
            jax.ShapeDtypeStruct((VISITS, 2, 8, 8, 128), jnp.bfloat16),
        ),
        in_specs=[vmem, vmem],
        out_specs=(vmem, vmem),
        scratch_shapes=[
            pltpu.VMEM((ROUNDS, n, 16, 128), jnp.bfloat16),
            pltpu.VMEM((n, 1, 128), jnp.int32),
            pltpu.VMEM((ROUNDS, n, 2, 8, 128), jnp.bfloat16),
            dma((ROUNDS,)),
            dma((ROUNDS,)),
            dma((ROUNDS,)),
            dma,
            dma,
            dma((ROUNDS,)),
            dma((ROUNDS,)),
            dma((VISITS, 2)),
            dma((VISITS, 2)),
        ],
        compiler_params=pltpu.CompilerParams(collective_id=0, has_side_effects=True),
        name="exchange",
    )(units, key_row)

    order, worder = orders()
    ctaps = basis[0].astype(jnp.float32)
    cbase = jnp.concatenate(
        [ctaps[:, 15::-1], jnp.zeros((BASIS, 128 - TAPS), jnp.float32), ctaps[:, :15:-1]], axis=1
    )
    rtaps = jnp.pad(basis[1].astype(jnp.float32), ((0, 1), (1, 64 - TAPS - 1)))
    rbase = rtaps.reshape(PAIRS, 128)
    coef = jnp.pad(spatial[0], ((0, 0), (0, 0), (0, 1)))
    coef = jnp.broadcast_to(coef[..., None], coef.shape + (64,)).reshape(VISITS, 3, DEPTH)
    coadd = pl.pallas_call(
        coadd_kernel,
        out_shape=jax.ShapeDtypeStruct((ROWS, COLS), jnp.float32),
        in_specs=[vmem] * 7,
        out_specs=vmem,
        scratch_shapes=[
            pltpu.VMEM((256, BASIS * 128), jnp.bfloat16),
            pltpu.VMEM((ROWS, DEPTH), jnp.float32),
            pltpu.VMEM((DEPTH, COLS), jnp.bfloat16),
            pltpu.VMEM((ROWS, COLS), jnp.float32),
            pltpu.VMEM((ROWS, COLS), jnp.float32),
        ],
        name="coadd",
    )(
        received,
        halo,
        jnp.asarray(order, jnp.bfloat16),
        jnp.asarray(worder, jnp.bfloat16),
        cbase,
        rbase,
        coef,
    )
    return coadd[None]


def solution(mesh):
    in_specs = (
        P(None, ("patch", "band"), None, None),
        P(None, ("patch", "band"), None, None),
        P(None, ("patch", "band")),
        P(None, ("patch", "band")),
        P(),
        P("patch", None, None, None),
    )
    out_specs = P("patch", "band", None)
    return jax.shard_map(
        per_device, mesh=mesh, in_specs=in_specs, out_specs=out_specs, check_vma=False
    )
```

```python
import jax
import jax.numpy as jnp
import numpy as np
from jax import lax
from jax.experimental import pallas as pl
from jax.experimental.pallas import tpu as pltpu
from jax.sharding import PartitionSpec as P

MESH = pl.DeviceIdType.MESH
VISITS = 6
BASIS = 21
TAPS = 31
ROWS = 32
COLS = 512
ROUNDS = 3
PAIRS = (BASIS + 1) // 2
DEPTH = PAIRS * 128
WIDE = PAIRS * 256


def bf16(value):
    return value.astype(jnp.bfloat16)


def iota(shape, dim):
    return lax.broadcasted_iota(jnp.int32, shape, dim)


def exact_dot(a, b):
    return jnp.dot(a, b, preferred_element_type=jnp.float32)


def one_hot(condition):
    return bf16(jnp.where(condition, 1.0, 0.0))


def kernel(flux_hbm, weight_hbm, patch_hbm, block_hbm, basis_hbm, spatial_hbm, order_hbm, worder_hbm,
           o_ref, tiles, dest, basis, spatial, both, order, worder, rows, key_row, y, keys, z, g, h,
           ctable, rtable, coefs, filtered, num, den,
           load, s1, s1b, r1, sk, rk, s2, r2, sh, rh):
    n, bands = lax.axis_size("patch"), lax.axis_size("band")
    me, band = lax.axis_index("patch"), lax.axis_index("band")
    chips = n // 2
    chip, core = me // 2, me % 2

    barrier = pltpu.get_barrier_semaphore()

    def greet(d, carry):
        pl.semaphore_signal(
            barrier, inc=1, device_id={"patch": (me + d) % n}, device_id_type=MESH
        )
        return carry

    lax.fori_loop(1, n, greet, 0)

    @pl.when(band > 0)
    def _():
        pl.semaphore_signal(barrier, inc=1, device_id={"band": band - 1}, device_id_type=MESH)

    @pl.when(band < bands - 1)
    def _():
        pl.semaphore_signal(barrier, inc=1, device_id={"band": band + 1}, device_id_type=MESH)

    loads = [
        pltpu.make_async_copy(source, target, load.at[i])
        for i, (source, target) in enumerate(
            (
                (patch_hbm, dest.at[0]),
                (block_hbm, dest.at[1]),
                (flux_hbm, tiles.at[0]),
                (weight_hbm, tiles.at[1]),
                (basis_hbm, basis),
                (spatial_hbm, spatial),
                (order_hbm, order),
                (worder_hbm, worder),
            )
        )
    ]
    for copy in loads:
        copy.start()

    loads[0].wait()
    loads[1].wait()
    spread = one_hot(iota((16, 128), 0) == iota((16, 128), 1) % 16)
    patch_lane = exact_dot(bf16(dest[0].astype(jnp.float32)), spread)
    block_lane = exact_dot(bf16(dest[1].astype(jnp.float32)), spread)
    mine = (iota((VISITS, 128), 0) + me) % 8 == iota((VISITS, 128), 1) // 16
    key_row[...] = jnp.sum(
        jnp.where(mine, patch_lane * 16.0 + block_lane, 0.0), axis=0, keepdims=True
    )
    turn = one_hot(
        (iota((128, 128), 0) % 16) * 8 + iota((128, 128), 0) // 16 == iota((128, 128), 1)
    )
    loads[2].wait()
    loads[3].wait()

    def turn_rows(visit, carry):
        for kind in range(2):
            pixels = bf16(
                jnp.concatenate(
                    [tiles[kind, visit, t].astype(jnp.float32) for t in range(16)], axis=0
                )
            )
            turned = bf16(exact_dot(turn, pixels))
            for r in range(8):
                rows[visit * 16 + kind * 8 + r] = turned[r * 16 : (r + 1) * 16]
        return carry

    lax.fori_loop(0, VISITS, turn_rows, 0)

    pl.semaphore_wait(
        barrier, n - 1 + (band + bands - 1) // bands + (2 * bands - 2 - band) // bands
    )

    def partner(i, count):
        half = (i + 1) // 2
        return count // 2 + half * (1 - 2 * (i % 2))

    def send_keys(i, carry):
        peer = (me + partner(i, n)) % n
        pltpu.make_async_remote_copy(
            key_row, keys.at[me], sk, rk, device_id={"patch": peer}, device_id_type=MESH
        ).start()
        return carry

    lax.fori_loop(0, n - 1, send_keys, 0)
    pltpu.make_async_copy(key_row, keys.at[me], rk).start()

    for q in range(ROUNDS):
        owner = q % 2

        def send_rows(i, carry):
            c = (chip + partner(i, chips)) % chips
            pltpu.make_async_remote_copy(
                rows.at[q * chips + c],
                y.at[q, me],
                s1.at[q],
                r1.at[q],
                device_id={"patch": 2 * c + owner},
                device_id_type=MESH,
            ).start()
            return carry

        lax.fori_loop(0, chips - 1, send_rows, 0)

        @pl.when(core == owner)
        def _():
            pltpu.make_async_copy(rows.at[q * chips + chip], y.at[q, me], r1.at[q]).start()

        @pl.when(core != owner)
        def _():
            pltpu.make_async_remote_copy(
                rows.at[q * chips + chip],
                y.at[q, me],
                s1b.at[q],
                r1.at[q],
                device_id={"patch": 2 * chip + owner},
                device_id_type=MESH,
            ).start()

    for copy in loads[4:]:
        copy.wait()
    tap, lane = iota((TAPS, 128), 0), iota((TAPS, 128), 1)
    for b in range(BASIS):
        both[2 * b : 2 * b + 2, 0:TAPS] = basis[b].astype(jnp.float32)
    taps_in = bf16(both[0 : 2 * BASIS, 0:TAPS])
    cbase = exact_dot(taps_in, one_hot((TAPS // 2 - tap + 128) % 128 == lane))
    rbase = [exact_dot(taps_in, one_hot(tap + 1 + 64 * odd == lane)) for odd in range(2)]
    near = jnp.abs(iota((128, 128), 0) - iota((128, 128), 1)) <= TAPS // 2
    for b in range(BASIS):
        taps = jnp.broadcast_to(cbase[2 * b : 2 * b + 1], (128, 128))
        cyclic = pltpu.roll(taps, 0, 1, stride=1, stride_axis=0)
        span = slice(b * 128, (b + 1) * 128)
        ctable[0:128, span] = bf16(jnp.where(near, cyclic, 0.0))
        ctable[128:256, span] = bf16(jnp.where(near, 0.0, cyclic))
    ctable[:, BASIS * 128 :] = jnp.zeros((256, WIDE - BASIS * 128), jnp.bfloat16)
    for pair in range(PAIRS):
        taps = rbase[0][4 * pair + 1 : 4 * pair + 2]
        if 2 * pair + 1 < BASIS:
            taps = taps + rbase[1][4 * pair + 3 : 4 * pair + 4]
        taps = jnp.broadcast_to(taps, (ROWS, 128))
        rtable[:, pair * 128 : (pair + 1) * 128] = pltpu.roll(taps, 0, 1, stride=1, stride_axis=0)
    widen = one_hot(iota((BASIS, DEPTH), 0) == iota((BASIS, DEPTH), 1) // 64)
    for visit in range(VISITS):
        for term in range(3):
            coefs[visit * 8 + term : visit * 8 + term + 1, 0:BASIS] = spatial[visit, term]
    plain = coefs[:, 0:BASIS]
    plain = jnp.where(iota(plain.shape, 0) % 8 < 3, plain, 0.0)
    top = bf16(plain)
    rest = plain - top.astype(jnp.float32)
    middle = bf16(rest)
    bottom = bf16(rest - middle.astype(jnp.float32))
    coefs[...] = exact_dot(top, widen) + exact_dot(middle, widen) + exact_dot(bottom, widen)
    num[...] = jnp.zeros_like(num)
    den[...] = jnp.zeros_like(den)

    pltpu.make_async_copy(keys, keys, rk).wait()

    def relay(q):
        group = iota((64, 128), 0) % 8
        lane_slot = iota((64, 128), 1) // 16
        table = keys[:, 0, :]
        options = []
        for visit in (2 * q, 2 * q + 1):
            picked = jnp.where((group + visit) % 8 == lane_slot, table, 0.0)
            picked = jnp.sum(picked.reshape(8, 8, 128), axis=1)
            options.append(pltpu.roll(picked, (128 - 16 * visit) % 128, 1))
        second = jnp.broadcast_to(chip // (chips // 2), (8, 128))
        wanted = jnp.where(second == 0, options[0], options[1]).astype(jnp.int32)
        pltpu.make_async_copy(y.at[q], y.at[q], r1.at[q]).wait()
        data = y[q].reshape(n * 16, 128)
        for part in range(4):
            place = iota((256, 128), 0) + 256 * part
            chosen = jnp.concatenate(
                [
                    one_hot(jnp.broadcast_to(wanted[k : k + 1], (256, 128)) == place)
                    for k in range(8)
                ],
                axis=1,
            )
            moved = exact_dot(chosen, data)
            z[q, part * 16 : (part + 1) * 16] = bf16(moved.reshape(16, 2, 8, 128))

        def send_blocks(i, carry):
            peer = (me + partner(i, n)) % n
            pltpu.make_async_remote_copy(
                z.at[q, peer],
                g.at[q * chips + chip],
                s2.at[q],
                r2.at[q],
                device_id={"patch": peer},
                device_id_type=MESH,
            ).start()
            return carry

        lax.fori_loop(0, n - 1, send_blocks, 0)
        pltpu.make_async_copy(z.at[q, me], g.at[q * chips + chip], r2.at[q]).start()

    @pl.when(core == 0)
    def _():
        relay(0)
        relay(2)

    @pl.when(core == 1)
    def _():
        relay(1)

    def halo(visit, side):
        half, step = (1, 1) if side == 0 else (0, -1)
        return pltpu.make_async_remote_copy(
            g.at[pl.ds(visit * 16, 8), half],
            h.at[visit, side],
            sh.at[visit, side],
            rh.at[visit, side],
            device_id={"band": band + step},
            device_id_type=MESH,
        )

    first = (band * ROWS).astype(jnp.float32)
    u = (2.0 * (iota((ROWS, 1), 0).astype(jnp.float32) + first) + 1.0) / (bands * ROWS) - 1.0
    w = (2.0 * iota((1, COLS), 1).astype(jnp.float32) + 1.0) / COLS - 1.0
    above_on = jnp.broadcast_to(band, (8, 128)) > 0
    below_on = jnp.broadcast_to(band, (8, 128)) < bands - 1
    left_lane = iota((256, 128), 1) < 64

    def one_visit(visit, carry):
        unit = visit * 16
        above = [jnp.where(above_on, h[visit, 0, r].astype(jnp.float32), 0.0) for r in range(8)]
        below = [jnp.where(below_on, h[visit, 1, r].astype(jnp.float32), 0.0) for r in range(8)]
        inner = [g[unit + r, half].astype(jnp.float32) for r in range(8) for half in range(2)]
        image = bf16(jnp.concatenate(above + inner + below, axis=0))
        moved = exact_dot(order[...], image)
        beside = jnp.where(left_lane, moved[256:512], moved[512:768])
        window = bf16(jnp.concatenate([moved[0:256], beside], axis=1))
        for pair in range(PAIRS):
            result = bf16(exact_dot(window, ctable[:, pair * 256 : (pair + 1) * 256]))
            for odd in range(2):
                b = 2 * pair + odd
                for c in range(4):
                    filtered[b * 64 : (b + 1) * 64, c * 128 : (c + 1) * 128] = result[
                        c * 64 : (c + 1) * 64, odd * 128 : (odd + 1) * 128
                    ]
        coef = coefs[pl.ds(pl.multiple_of(visit * 8, 8), 8)]
        table = rtable[...]
        steady = table * (coef[0:1] + u * coef[1:2])
        slope = table * coef[2:3]
        full = jnp.concatenate([steady, slope], axis=0)
        high = bf16(full)
        low = bf16(full - high.astype(jnp.float32))
        mixed = exact_dot(jnp.concatenate([high, low], axis=0), filtered[...])
        mixed = mixed[0:64] + mixed[64:128]
        matched = mixed[0:ROWS] + w * mixed[ROWS:64]
        weights = [g[unit + 8 + r, half].astype(jnp.float32) for r in range(8) for half in range(2)]
        weights = exact_dot(worder[...], bf16(jnp.concatenate(weights, axis=0)))
        weights = jnp.concatenate([weights[c * ROWS : (c + 1) * ROWS] for c in range(4)], axis=1)
        num[...] += weights * matched
        den[...] += weights
        return carry

    def share_edges(q):
        part = g.at[pl.ds(q * chips, chips)]
        pltpu.make_async_copy(part, part, r2.at[q]).wait()

        @pl.when(band < bands - 1)
        def _():
            halo(2 * q, 0).start()
            halo(2 * q + 1, 0).start()

        @pl.when(band > 0)
        def _():
            halo(2 * q, 1).start()
            halo(2 * q + 1, 1).start()

    def wait_edges(q):
        @pl.when(band < bands - 1)
        def _():
            halo(2 * q, 1).wait_recv()
            halo(2 * q + 1, 1).wait_recv()

        @pl.when(band > 0)
        def _():
            halo(2 * q, 0).wait_recv()
            halo(2 * q + 1, 0).wait_recv()

    share_edges(0)
    share_edges(1)
    wait_edges(0)
    wait_edges(1)
    lax.fori_loop(0, 3, one_visit, 0)
    share_edges(2)
    lax.fori_loop(3, 4, one_visit, 0)
    wait_edges(2)
    lax.fori_loop(4, 6, one_visit, 0)
    o_ref[...] = num[...] / den[...]

    @pl.when(band < bands - 1)
    def _():
        for visit in range(VISITS):
            halo(visit, 0).wait_send()

    @pl.when(band > 0)
    def _():
        for visit in range(VISITS):
            halo(visit, 1).wait_send()

    pltpu.make_async_copy(keys.at[pl.ds(0, n - 1)], keys.at[pl.ds(0, n - 1)], sk).wait()
    for q in range(ROUNDS):
        owner = q % 2
        sent = rows.at[pl.ds(0, chips - 1)]
        pltpu.make_async_copy(sent, sent, s1.at[q]).wait()

        @pl.when(core != owner)
        def _():
            pltpu.make_async_copy(rows.at[0], rows.at[0], s1b.at[q]).wait()

        @pl.when(core == owner)
        def _():
            relayed = z.at[q, pl.ds(0, n - 1)]
            pltpu.make_async_copy(relayed, relayed, s2.at[q]).wait()


def orders():
    order = np.zeros((3, 4, 64, 256), np.float32)
    for c in range(4):
        for t in range(64):
            for kind, shift in ((0, 0), (1, 1), (2, -1)):
                d = c + shift
                if not 0 <= d < 4:
                    continue
                if t < 16:
                    place = (t % 8) * 8 + (t // 8) * 4 + d
                elif t < 48:
                    s = t - 16
                    place = 64 + (s % 8) * 16 + (s // 8) * 4 + d
                else:
                    s = t - 48
                    place = 192 + (s % 8) * 8 + (s // 8) * 4 + d
                order[kind, c, t, place] = 1.0
    worder = np.zeros((4, ROWS, 128), np.float32)
    for c in range(4):
        for s in range(ROWS):
            worder[c, s, (s % 8) * 16 + (s // 8) * 4 + c] = 1.0
    return order.reshape(768, 256), worder.reshape(128, 128)


def per_device(tile_flux, tile_weight, dest_patch, dest_block, basis, spatial):
    n = lax.axis_size("patch")
    vmem, dma = pltpu.VMEM, pltpu.SemaphoreType.DMA
    order, worder = orders()
    coadd = pl.pallas_call(
        kernel,
        out_shape=jax.ShapeDtypeStruct((ROWS, COLS), jnp.float32),
        in_specs=[pl.BlockSpec(memory_space=pl.ANY)] * 8,
        out_specs=pl.BlockSpec(memory_space=vmem),
        scratch_shapes=[
            vmem((2, VISITS, 16, 8, 128), jnp.bfloat16),
            vmem((2, VISITS, 16), jnp.int32),
            vmem((BASIS, 2, TAPS), jnp.bfloat16),
            vmem((VISITS, 3, 1, BASIS), jnp.float32),
            vmem((48, 128), jnp.float32),
            vmem((768, 256), jnp.bfloat16),
            vmem((128, 128), jnp.bfloat16),
            vmem((VISITS * 16, 16, 128), jnp.bfloat16),
            vmem((1, 128), jnp.float32),
            vmem((ROUNDS, n, 16, 128), jnp.bfloat16),
            vmem((n, 1, 128), jnp.float32),
            vmem((ROUNDS, n, 2, 8, 128), jnp.bfloat16),
            vmem((VISITS * 16, 2, 8, 128), jnp.bfloat16),
            vmem((VISITS, 2, 8, 8, 128), jnp.bfloat16),
            vmem((256, WIDE), jnp.bfloat16),
            vmem((ROWS, DEPTH), jnp.float32),
            vmem((VISITS * 8, DEPTH), jnp.float32),
            vmem((DEPTH, COLS), jnp.bfloat16),
            vmem((ROWS, COLS), jnp.float32),
            vmem((ROWS, COLS), jnp.float32),
            dma((8,)),
            dma((ROUNDS,)),
            dma((ROUNDS,)),
            dma((ROUNDS,)),
            dma,
            dma,
            dma((ROUNDS,)),
            dma((ROUNDS,)),
            dma((VISITS, 2)),
            dma((VISITS, 2)),
        ],
        compiler_params=pltpu.CompilerParams(collective_id=0, has_side_effects=True),
        name="coadd",
    )(
        tile_flux,
        tile_weight,
        dest_patch,
        dest_block,
        basis.transpose(1, 0, 2),
        spatial.transpose(1, 2, 0, 3),
        jnp.asarray(order, jnp.bfloat16),
        jnp.asarray(worder, jnp.bfloat16),
    )
    return coadd[None]


def solution(mesh):
    in_specs = (
        P(None, ("patch", "band"), None, None),
        P(None, ("patch", "band"), None, None),
        P(None, ("patch", "band")),
        P(None, ("patch", "band")),
        P(),
        P("patch", None, None, None),
    )
    out_specs = P("patch", "band", None)
    return jax.shard_map(
        per_device, mesh=mesh, in_specs=in_specs, out_specs=out_specs, check_vma=False
    )
```

```python
import jax
import jax.numpy as jnp
import numpy as np
from jax import lax
from jax.experimental import pallas as pl
from jax.experimental.pallas import tpu as pltpu
from jax.sharding import PartitionSpec as P

MESH = pl.DeviceIdType.MESH
VISITS = 6
BASIS = 21
TAPS = 31
ROWS = 32
COLS = 512
NEAR = 4
AHEAD = 3
ROUNDS = 6
LEVELS = ((4, 0), (0, ROUNDS))
PAIRS = (BASIS + 1) // 2
DEPTH = PAIRS * 128
WIDE = PAIRS * 256


def bf16(value):
    return value.astype(jnp.bfloat16)


def iota(shape, dim):
    return lax.broadcasted_iota(jnp.int32, shape, dim)


def exact_dot(a, b):
    return jnp.dot(a, b, preferred_element_type=jnp.float32)


def one_hot(condition):
    return bf16(jnp.where(condition, 1.0, 0.0))


def kernel(flux_hbm, weight_hbm, patch_hbm, block_hbm, basis_hbm, spatial_hbm, order_hbm, worder_hbm,
           o_ref, tiles, dest, basis, spatial, both, order, worder, rows, key_row, y, keys, z, g, h,
           ctable, rtable, coefs, filtered, matched, num, den,
           load, heard, s1, s1b, r1, sk, rk, sk4, rk4, s2, r2, sh, rh):
    n, bands = lax.axis_size("patch"), lax.axis_size("band")
    me, band = lax.axis_index("patch"), lax.axis_index("band")
    core = me % 2

    zs = n // 4
    height, lane4 = me // 4, me % 4

    def peer_at(step, place):
        return ((height + step + zs) % zs) * 4 + place

    barrier = pltpu.get_barrier_semaphore()

    def greet(i, carry):
        peer = peer_at(i // 4 - NEAR, i % 4)
        pl.semaphore_signal(barrier, inc=1, device_id={"patch": peer}, device_id_type=MESH)
        return carry

    lax.fori_loop(0, NEAR * 4, greet, 0)
    lax.fori_loop(NEAR * 4 + 4, NEAR * 8 + 4, greet, 0)
    for d in range(1, 4):
        peer = peer_at(0, (lane4 + d) % 4)
        pl.semaphore_signal(barrier, inc=1, device_id={"patch": peer}, device_id_type=MESH)

    @pl.when(band > 0)
    def _():
        pl.semaphore_signal(barrier, inc=1, device_id={"band": band - 1}, device_id_type=MESH)

    @pl.when(band < bands - 1)
    def _():
        pl.semaphore_signal(barrier, inc=1, device_id={"band": band + 1}, device_id_type=MESH)

    loads = [
        pltpu.make_async_copy(source, target, load.at[i])
        for i, (source, target) in enumerate(
            (
                (patch_hbm, dest.at[0]),
                (block_hbm, dest.at[1]),
                (flux_hbm, tiles.at[0]),
                (weight_hbm, tiles.at[1]),
                (basis_hbm, basis),
                (spatial_hbm, spatial),
                (order_hbm, order),
                (worder_hbm, worder),
            )
        )
    ]
    for copy in loads:
        copy.start()

    loads[0].wait()
    loads[1].wait()
    spread = one_hot(iota((16, 128), 0) == iota((16, 128), 1) % 16)
    patch_lane = exact_dot(bf16(dest[0].astype(jnp.float32)), spread)
    block_lane = exact_dot(bf16(dest[1].astype(jnp.float32)), spread)
    key_lane = patch_lane * 16.0 + block_lane
    key_lane = jnp.where(iota((VISITS, 128), 0) == iota((VISITS, 128), 1) // 16, key_lane, 0.0)
    key_row[...] = jnp.sum(key_lane, axis=0, keepdims=True)
    turn = one_hot(
        (iota((128, 128), 0) % 16) * 8 + iota((128, 128), 0) // 16 == iota((128, 128), 1)
    )
    loads[2].wait()
    loads[3].wait()

    def turn_rows(visit, carry):
        for kind in range(2):
            pixels = bf16(
                jnp.concatenate(
                    [tiles[kind, visit, t].astype(jnp.float32) for t in range(16)], axis=0
                )
            )
            turned = bf16(exact_dot(turn, pixels))
            for r in range(8):
                rows[kind * VISITS * 8 + visit * 8 + r] = turned[r * 16 : (r + 1) * 16]
        return carry

    lax.fori_loop(0, VISITS, turn_rows, 0)

    pl.semaphore_wait(
        barrier, NEAR * 8 + 3 + (band + bands - 1) // bands + (2 * bands - 2 - band) // bands
    )

    def send_key(step):
        pltpu.make_async_remote_copy(
            key_row,
            keys.at[lane4, height],
            sk,
            rk,
            device_id={"patch": peer_at(step, lane4)},
            device_id_type=MESH,
        ).start()

    def send_row(turn_no, step):
        place = (turn_no % 2) * 2 + (turn_no // 2) % 2
        pltpu.make_async_remote_copy(
            rows.at[turn_no * 16 + (height + step + zs) % zs],
            y.at[turn_no // 4, me],
            s1.at[turn_no],
            r1.at[turn_no // 4],
            device_id={"patch": peer_at(step, place)},
            device_id_type=MESH,
        ).start()

    def send_ring(inner, outer, rounds, with_keys):
        def one(i, carry):
            reach = outer - i
            for step in (reach, -reach):
                if with_keys:
                    send_key(step)
                for turn_no in rounds:
                    send_row(turn_no, step)
            return carry

        lax.fori_loop(0, outer - inner, one, 0)
        if outer == zs // 2 - 1:
            if with_keys:
                send_key(zs // 2)
            for turn_no in rounds:
                send_row(turn_no, zs // 2)

    pltpu.make_async_copy(key_row, keys.at[lane4, height], rk).start()

    def own_height(rounds):
        for turn_no in rounds:
            place = (turn_no % 2) * 2 + (turn_no // 2) % 2

            @pl.when(lane4 == place)
            def _():
                pltpu.make_async_copy(
                    rows.at[turn_no * 16 + height], y.at[turn_no // 4, me], r1.at[turn_no // 4]
                ).start()

            @pl.when(lane4 != place)
            def _():
                pltpu.make_async_remote_copy(
                    rows.at[turn_no * 16 + height],
                    y.at[turn_no // 4, me],
                    s1b.at[turn_no],
                    r1.at[turn_no // 4],
                    device_id={"patch": peer_at(0, place)},
                    device_id_type=MESH,
                ).start()

    known, sent = NEAR, [0] * ROUNDS
    for level, (reach, count) in enumerate(LEVELS):
        if reach:
            for step in (reach, -reach):
                pl.semaphore_signal(
                    heard.at[level],
                    inc=1,
                    device_id={"patch": peer_at(step, lane4)},
                    device_id_type=MESH,
                )
        if level == 0:
            send_ring(0, known, (0,), True)
            if AHEAD > 1:
                send_ring(0, known, tuple(range(1, AHEAD)), False)
            own_height(range(ROUNDS))
            sent = [known] * AHEAD + [0] * (ROUNDS - AHEAD)
        else:
            for turn_no in range(count):
                send_ring(sent[turn_no], known, (turn_no,), sent[turn_no] == before and turn_no == 0)
                sent[turn_no] = known
        before = known
        if reach:
            pl.semaphore_wait(heard.at[level], 2)
            known = min(known + reach, zs // 2 - 1)

    column = keys.at[lane4]
    pltpu.make_async_copy(column, column, rk).wait()

    def forward(d):
        return pltpu.make_async_remote_copy(
            column,
            keys.at[lane4],
            sk4.at[d - 1],
            rk4.at[d - 1],
            device_id={"patch": peer_at(0, (lane4 + d) % 4)},
            device_id_type=MESH,
        )

    for d in range(1, 4):
        forward(d).start()

    for copy in loads[4:]:
        copy.wait()
    tap, lane = iota((TAPS, 128), 0), iota((TAPS, 128), 1)
    for b in range(BASIS):
        both[2 * b : 2 * b + 2, 0:TAPS] = basis[b].astype(jnp.float32)
    taps_in = bf16(both[0 : 2 * BASIS, 0:TAPS])
    cbase = exact_dot(taps_in, one_hot((TAPS // 2 - tap + 128) % 128 == lane))
    rbase = [exact_dot(taps_in, one_hot(tap + 1 + 64 * odd == lane)) for odd in range(2)]
    near = jnp.abs(iota((128, 128), 0) - iota((128, 128), 1)) <= TAPS // 2
    for b in range(BASIS):
        taps = jnp.broadcast_to(cbase[2 * b : 2 * b + 1], (128, 128))
        cyclic = pltpu.roll(taps, 0, 1, stride=1, stride_axis=0)
        span = slice(b * 128, (b + 1) * 128)
        ctable[0:128, span] = bf16(jnp.where(near, cyclic, 0.0))
        ctable[128:256, span] = bf16(jnp.where(near, 0.0, cyclic))
    ctable[:, BASIS * 128 :] = jnp.zeros((256, WIDE - BASIS * 128), jnp.bfloat16)
    for pair in range(PAIRS):
        taps = rbase[0][4 * pair + 1 : 4 * pair + 2]
        if 2 * pair + 1 < BASIS:
            taps = taps + rbase[1][4 * pair + 3 : 4 * pair + 4]
        taps = jnp.broadcast_to(taps, (ROWS, 128))
        rtable[:, pair * 128 : (pair + 1) * 128] = pltpu.roll(taps, 0, 1, stride=1, stride_axis=0)
    widen = one_hot(iota((BASIS, DEPTH), 0) == iota((BASIS, DEPTH), 1) // 64)
    for visit in range(VISITS):
        for term in range(3):
            coefs[visit * 8 + term : visit * 8 + term + 1, 0:BASIS] = spatial[visit, term]
    plain = coefs[:, 0:BASIS]
    plain = jnp.where(iota(plain.shape, 0) % 8 < 3, plain, 0.0)
    top = bf16(plain)
    rest = plain - top.astype(jnp.float32)
    middle = bf16(rest)
    bottom = bf16(rest - middle.astype(jnp.float32))
    coefs[...] = exact_dot(top, widen) + exact_dot(middle, widen) + exact_dot(bottom, widen)
    num[...] = jnp.zeros_like(num)
    den[...] = jnp.zeros_like(den)

    for d in range(1, 4):
        forward(d).wait_recv()

    def partner(i):
        half = (i + 1) // 2
        return n // 2 + half * (1 - 2 * (i % 2))

    def relay(slot):
        turn_no = me // 2 % 2 + 2 * core if slot == 0 else me // 2 % 2 + 4
        visit = 2 * (turn_no % 3) + height // 8
        table = keys[...].reshape(64, 128)
        patch_of = jnp.floor(table * (1.0 / 16.0))
        block_of = table - 16.0 * patch_of
        spread = one_hot(iota((128, 128), 0) == iota((128, 128), 1) % 16 + 16 * visit)
        source = iota((64, 128), 0) % 16 % 2 * 4 + iota((64, 128), 0) // 16
        held = source == iota((64, 128), 1) // 16
        gather = one_hot(iota((8, 64), 1) % 16 // 2 == iota((8, 64), 0))
        patch_of = jnp.where(held, exact_dot(bf16(patch_of), spread), 0.0)
        block_of = jnp.where(held, exact_dot(bf16(block_of), spread), 0.0)
        wanted = exact_dot(gather, bf16(patch_of)) * 16.0 + exact_dot(gather, bf16(block_of))
        wanted = wanted.astype(jnp.int32)
        pltpu.make_async_copy(y.at[slot], y.at[slot], r1.at[slot]).wait()
        data = y[slot].reshape(n * 16, 128)
        for part in range(4):
            place = iota((256, 128), 0) + 256 * part
            chosen = jnp.concatenate(
                [
                    one_hot(jnp.broadcast_to(wanted[k : k + 1], (256, 128)) == place)
                    for k in range(8)
                ],
                axis=1,
            )
            moved = exact_dot(chosen, data)
            z[slot, part * 16 : (part + 1) * 16] = bf16(moved.reshape(16, 2, 8, 128))

        def send_blocks(i, carry):
            peer = (me + partner(i)) % n
            pltpu.make_async_remote_copy(
                z.at[slot, peer],
                g.at[turn_no * 16 + height],
                s2.at[slot],
                r2.at[turn_no],
                device_id={"patch": peer},
                device_id_type=MESH,
            ).start()
            return carry

        lax.fori_loop(0, n - 1, send_blocks, 0)
        pltpu.make_async_copy(z.at[slot, me], g.at[turn_no * 16 + height], r2.at[turn_no]).start()

    relay(0)

    @pl.when(core == 0)
    def _():
        relay(1)

    def halo(visit, side):
        half, step = (1, 1) if side == 0 else (0, -1)
        return pltpu.make_async_remote_copy(
            g.at[pl.ds(visit * 8, 8), half],
            h.at[visit, side],
            sh.at[visit, side],
            rh.at[visit, side],
            device_id={"band": band + step},
            device_id_type=MESH,
        )

    first = (band * ROWS).astype(jnp.float32)
    u = (2.0 * (iota((ROWS, 1), 0).astype(jnp.float32) + first) + 1.0) / (bands * ROWS) - 1.0
    w = (2.0 * iota((1, COLS), 1).astype(jnp.float32) + 1.0) / COLS - 1.0
    above_on = jnp.broadcast_to(band, (8, 128)) > 0
    below_on = jnp.broadcast_to(band, (8, 128)) < bands - 1
    left_lane = iota((256, 128), 1) < 64

    def one_visit(visit, carry):
        unit = visit * 8
        above = [jnp.where(above_on, h[visit, 0, r].astype(jnp.float32), 0.0) for r in range(8)]
        below = [jnp.where(below_on, h[visit, 1, r].astype(jnp.float32), 0.0) for r in range(8)]
        inner = [g[unit + r, half].astype(jnp.float32) for r in range(8) for half in range(2)]
        image = bf16(jnp.concatenate(above + inner + below, axis=0))
        moved = exact_dot(order[...], image)
        beside = jnp.where(left_lane, moved[256:512], moved[512:768])
        window = bf16(jnp.concatenate([moved[0:256], beside], axis=1))
        for pair in range(PAIRS):
            result = bf16(exact_dot(window, ctable[:, pair * 256 : (pair + 1) * 256]))
            for odd in range(2):
                b = 2 * pair + odd
                for c in range(4):
                    filtered[b * 64 : (b + 1) * 64, c * 128 : (c + 1) * 128] = result[
                        c * 64 : (c + 1) * 64, odd * 128 : (odd + 1) * 128
                    ]
        coef = coefs[pl.ds(pl.multiple_of(visit * 8, 8), 8)]
        table = rtable[...]
        steady = table * (coef[0:1] + u * coef[1:2])
        slope = table * coef[2:3]
        full = jnp.concatenate([steady, slope], axis=0)
        high = bf16(full)
        low = bf16(full - high.astype(jnp.float32))
        mixed = exact_dot(jnp.concatenate([high, low], axis=0), filtered[...])
        mixed = mixed[0:64] + mixed[64:128]
        matched[visit] = mixed[0:ROWS] + w * mixed[ROWS:64]
        return carry

    def weigh(visit, carry):
        unit = (VISITS + visit) * 8
        weights = [g[unit + r, half].astype(jnp.float32) for r in range(8) for half in range(2)]
        weights = exact_dot(worder[...], bf16(jnp.concatenate(weights, axis=0)))
        weights = jnp.concatenate([weights[c * ROWS : (c + 1) * ROWS] for c in range(4)], axis=1)
        num[...] += weights * matched[visit]
        den[...] += weights
        return carry

    def arrived(turn_no):
        part = g.at[pl.ds(turn_no * 16, 16)]
        pltpu.make_async_copy(part, part, r2.at[turn_no]).wait()

    def share_edges(turn_no):
        arrived(turn_no)

        @pl.when(band < bands - 1)
        def _():
            halo(2 * turn_no, 0).start()
            halo(2 * turn_no + 1, 0).start()

        @pl.when(band > 0)
        def _():
            halo(2 * turn_no, 1).start()
            halo(2 * turn_no + 1, 1).start()

    def filter_pair(turn_no, carry):
        @pl.when(turn_no < 2)
        def _():
            share_edges(turn_no + 1)

        @pl.when(band < bands - 1)
        def _():
            halo(2 * turn_no, 1).wait_recv()
            halo(2 * turn_no + 1, 1).wait_recv()

        @pl.when(band > 0)
        def _():
            halo(2 * turn_no, 0).wait_recv()
            halo(2 * turn_no + 1, 0).wait_recv()

        return lax.fori_loop(2 * turn_no, 2 * turn_no + 2, one_visit, carry)

    def weigh_pair(turn_no, carry):
        arrived(turn_no + 3)
        return lax.fori_loop(2 * turn_no, 2 * turn_no + 2, weigh, carry)

    share_edges(0)
    lax.fori_loop(0, 3, filter_pair, 0)
    lax.fori_loop(0, 3, weigh_pair, 0)
    o_ref[...] = num[...] / den[...]

    @pl.when(band < bands - 1)
    def _():
        for visit in range(VISITS):
            halo(visit, 0).wait_send()

    @pl.when(band > 0)
    def _():
        for visit in range(VISITS):
            halo(visit, 1).wait_send()

    told = keys.at[0, pl.ds(0, zs - 1)]
    pltpu.make_async_copy(told, told, sk).wait()
    for d in range(1, 4):
        forward(d).wait_send()
    for visit in range(VISITS):
        gone = rows.at[pl.ds(0, zs - 1)]
        pltpu.make_async_copy(gone, gone, s1.at[visit]).wait()

        @pl.when(lane4 != (visit % 2) * 2 + (visit // 2) % 2)
        def _():
            pltpu.make_async_copy(rows.at[0], rows.at[0], s1b.at[visit]).wait()

    relayed = z.at[0, pl.ds(0, n - 1)]
    pltpu.make_async_copy(relayed, relayed, s2.at[0]).wait()

    @pl.when(core == 0)
    def _():
        pltpu.make_async_copy(relayed, relayed, s2.at[1]).wait()


def orders():
    order = np.zeros((3, 4, 64, 256), np.float32)
    for c in range(4):
        for t in range(64):
            for kind, shift in ((0, 0), (1, 1), (2, -1)):
                d = c + shift
                if not 0 <= d < 4:
                    continue
                if t < 16:
                    place = (t % 8) * 8 + (t // 8) * 4 + d
                elif t < 48:
                    s = t - 16
                    place = 64 + (s % 8) * 16 + (s // 8) * 4 + d
                else:
                    s = t - 48
                    place = 192 + (s % 8) * 8 + (s // 8) * 4 + d
                order[kind, c, t, place] = 1.0
    worder = np.zeros((4, ROWS, 128), np.float32)
    for c in range(4):
        for s in range(ROWS):
            worder[c, s, (s % 8) * 16 + (s // 8) * 4 + c] = 1.0
    return order.reshape(768, 256), worder.reshape(128, 128)


def per_device(tile_flux, tile_weight, dest_patch, dest_block, basis, spatial):
    n = lax.axis_size("patch")
    vmem, dma = pltpu.VMEM, pltpu.SemaphoreType.DMA
    order, worder = orders()
    coadd = pl.pallas_call(
        kernel,
        out_shape=jax.ShapeDtypeStruct((ROWS, COLS), jnp.float32),
        in_specs=[pl.BlockSpec(memory_space=pl.ANY)] * 8,
        out_specs=pl.BlockSpec(memory_space=vmem),
        scratch_shapes=[
            vmem((2, VISITS, 16, 8, 128), jnp.bfloat16),
            vmem((2, VISITS, 16), jnp.int32),
            vmem((BASIS, 2, TAPS), jnp.bfloat16),
            vmem((VISITS, 3, 1, BASIS), jnp.float32),
            vmem((48, 128), jnp.float32),
            vmem((768, 256), jnp.bfloat16),
            vmem((128, 128), jnp.bfloat16),
            vmem((VISITS * 16, 16, 128), jnp.bfloat16),
            vmem((1, 128), jnp.float32),
            vmem((2, n, 16, 128), jnp.bfloat16),
            vmem((4, n // 4, 1, 128), jnp.float32),
            vmem((2, n, 2, 8, 128), jnp.bfloat16),
            vmem((VISITS * 16, 2, 8, 128), jnp.bfloat16),
            vmem((VISITS, 2, 8, 8, 128), jnp.bfloat16),
            vmem((256, WIDE), jnp.bfloat16),
            vmem((ROWS, DEPTH), jnp.float32),
            vmem((VISITS * 8, DEPTH), jnp.float32),
            vmem((DEPTH, COLS), jnp.bfloat16),
            vmem((VISITS, ROWS, COLS), jnp.float32),
            vmem((ROWS, COLS), jnp.float32),
            vmem((ROWS, COLS), jnp.float32),
            dma((8,)),
            pltpu.SemaphoreType.REGULAR((len(LEVELS),)),
            dma((VISITS,)),
            dma((VISITS,)),
            dma((2,)),
            dma,
            dma,
            dma((3,)),
            dma((3,)),
            dma((2,)),
            dma((VISITS,)),
            dma((VISITS, 2)),
            dma((VISITS, 2)),
        ],
        compiler_params=pltpu.CompilerParams(collective_id=0, has_side_effects=True),
        name="coadd",
    )(
        tile_flux,
        tile_weight,
        dest_patch,
        dest_block,
        basis.transpose(1, 0, 2),
        spatial.transpose(1, 2, 0, 3),
        jnp.asarray(order, jnp.bfloat16),
        jnp.asarray(worder, jnp.bfloat16),
    )
    return coadd[None]


def solution(mesh):
    in_specs = (
        P(None, ("patch", "band"), None, None),
        P(None, ("patch", "band"), None, None),
        P(None, ("patch", "band")),
        P(None, ("patch", "band")),
        P(),
        P("patch", None, None, None),
    )
    out_specs = P("patch", "band", None)
    return jax.shard_map(
        per_device, mesh=mesh, in_specs=in_specs, out_specs=out_specs, check_vma=False
    )
```

```python
import jax
import jax.numpy as jnp
import numpy as np
from jax import lax
from jax.experimental import pallas as pl
from jax.experimental.pallas import tpu as pltpu
from jax.sharding import PartitionSpec as P

MESH = pl.DeviceIdType.MESH
VISITS = 6
BASIS = 21
TAPS = 31
ROWS = 32
COLS = 512
NEAR = 4
AHEAD = 3
ROUNDS = 6
P1ORDER = (0, 1, 2, 4, 5, 3)
LEVELS = ((4, 0), (0, ROUNDS))
PAIRS = (BASIS + 1) // 2
DEPTH = PAIRS * 128
WIDE = PAIRS * 256


def bf16(value):
    return value.astype(jnp.bfloat16)


def iota(shape, dim):
    return lax.broadcasted_iota(jnp.int32, shape, dim)


def exact_dot(a, b):
    return jnp.dot(a, b, preferred_element_type=jnp.float32)


def one_hot(condition):
    return bf16(jnp.where(condition, 1.0, 0.0))


def kernel(flux_hbm, weight_hbm, patch_hbm, block_hbm, basis_hbm, spatial_hbm, order_hbm, worder_hbm,
           o_ref, tiles, dest, basis, spatial, both, order, worder, rows, key_row, y, keys, z, g, h,
           ctable, rtable, coefs, filtered, matched, num, den,
           load, heard, s1, s1b, r1, sk, rk, sk4, rk4, s2, r2, sh, rh):
    n, bands = lax.axis_size("patch"), lax.axis_size("band")
    me, band = lax.axis_index("patch"), lax.axis_index("band")
    core = me % 2

    zs = n // 4
    height, lane4 = me // 4, me % 4

    def peer_at(step, place):
        return ((height + step + zs) % zs) * 4 + place

    barrier = pltpu.get_barrier_semaphore()

    def greet(i, carry):
        peer = peer_at(i // 4 - NEAR, i % 4)
        pl.semaphore_signal(barrier, inc=1, device_id={"patch": peer}, device_id_type=MESH)
        return carry

    lax.fori_loop(0, NEAR * 4, greet, 0)
    lax.fori_loop(NEAR * 4 + 4, NEAR * 8 + 4, greet, 0)
    for d in range(1, 4):
        peer = peer_at(0, (lane4 + d) % 4)
        pl.semaphore_signal(barrier, inc=1, device_id={"patch": peer}, device_id_type=MESH)

    @pl.when(band > 0)
    def _():
        pl.semaphore_signal(barrier, inc=1, device_id={"band": band - 1}, device_id_type=MESH)

    @pl.when(band < bands - 1)
    def _():
        pl.semaphore_signal(barrier, inc=1, device_id={"band": band + 1}, device_id_type=MESH)

    loads = [
        pltpu.make_async_copy(source, target, load.at[i])
        for i, (source, target) in enumerate(
            (
                (patch_hbm, dest.at[0]),
                (block_hbm, dest.at[1]),
                (flux_hbm, tiles.at[0]),
                (weight_hbm, tiles.at[1]),
                (basis_hbm, basis),
                (spatial_hbm, spatial),
                (order_hbm, order),
                (worder_hbm, worder),
            )
        )
    ]
    for copy in loads:
        copy.start()

    loads[0].wait()
    loads[1].wait()
    spread = one_hot(iota((16, 128), 0) == iota((16, 128), 1) % 16)
    patch_lane = exact_dot(bf16(dest[0].astype(jnp.float32)), spread)
    block_lane = exact_dot(bf16(dest[1].astype(jnp.float32)), spread)
    key_lane = patch_lane * 16.0 + block_lane
    key_lane = jnp.where(iota((VISITS, 128), 0) == iota((VISITS, 128), 1) // 16, key_lane, 0.0)
    key_row[...] = jnp.sum(key_lane, axis=0, keepdims=True)
    turn = one_hot(
        (iota((128, 128), 0) % 16) * 8 + iota((128, 128), 0) // 16 == iota((128, 128), 1)
    )
    loads[2].wait()
    loads[3].wait()

    def turn_rows(visit, carry):
        for kind in range(2):
            pixels = bf16(
                jnp.concatenate(
                    [tiles[kind, visit, t].astype(jnp.float32) for t in range(16)], axis=0
                )
            )
            turned = bf16(exact_dot(turn, pixels))
            for r in range(8):
                rows[kind * VISITS * 8 + visit * 8 + r] = turned[r * 16 : (r + 1) * 16]
        return carry

    lax.fori_loop(0, VISITS, turn_rows, 0)

    pl.semaphore_wait(
        barrier, NEAR * 8 + 3 + (band + bands - 1) // bands + (2 * bands - 2 - band) // bands
    )

    def send_key(step):
        pltpu.make_async_remote_copy(
            key_row,
            keys.at[lane4, height],
            sk,
            rk,
            device_id={"patch": peer_at(step, lane4)},
            device_id_type=MESH,
        ).start()

    def place_of(turn_no, at):
        if turn_no in (2, 3):
            return (at + turn_no) % 2 * 2 + 1
        return turn_no % 2 * 2

    def send_row(turn_no, step):
        place = place_of(turn_no, height + step + zs)
        pltpu.make_async_remote_copy(
            rows.at[turn_no * 16 + (height + step + zs) % zs],
            y.at[turn_no // 4, me],
            s1.at[turn_no],
            r1.at[turn_no // 4],
            device_id={"patch": peer_at(step, place)},
            device_id_type=MESH,
        ).start()

    def send_ring(inner, outer, rounds, with_keys):
        def one(i, carry):
            reach = outer - i
            for step in (reach, -reach):
                if with_keys:
                    send_key(step)
                for turn_no in rounds:
                    send_row(turn_no, step)
            return carry

        lax.fori_loop(0, outer - inner, one, 0)
        if outer == zs // 2 - 1:
            if with_keys:
                send_key(zs // 2)
            for turn_no in rounds:
                send_row(turn_no, zs // 2)

    pltpu.make_async_copy(key_row, keys.at[lane4, height], rk).start()

    def own_height(rounds):
        for turn_no in rounds:
            place = place_of(turn_no, height)

            @pl.when(lane4 == place)
            def _():
                pltpu.make_async_copy(
                    rows.at[turn_no * 16 + height], y.at[turn_no // 4, me], r1.at[turn_no // 4]
                ).start()

            @pl.when(lane4 != place)
            def _():
                pltpu.make_async_remote_copy(
                    rows.at[turn_no * 16 + height],
                    y.at[turn_no // 4, me],
                    s1b.at[turn_no],
                    r1.at[turn_no // 4],
                    device_id={"patch": peer_at(0, place)},
                    device_id_type=MESH,
                ).start()

    known, sent = NEAR, [0] * ROUNDS
    for level, (reach, count) in enumerate(LEVELS):
        if reach:
            for step in (reach, -reach):
                pl.semaphore_signal(
                    heard.at[level],
                    inc=1,
                    device_id={"patch": peer_at(step, lane4)},
                    device_id_type=MESH,
                )
        if level == 0:
            send_ring(0, known, (0,), True)
            if AHEAD > 1:
                send_ring(0, known, tuple(range(1, AHEAD)), False)
            own_height(range(ROUNDS))
            sent = [known] * AHEAD + [0] * (ROUNDS - AHEAD)
        else:
            for turn_no in P1ORDER[:count]:
                send_ring(sent[turn_no], known, (turn_no,), sent[turn_no] == before and turn_no == 0)
                sent[turn_no] = known
        before = known
        if reach:
            pl.semaphore_wait(heard.at[level], 2)
            known = min(known + reach, zs // 2 - 1)

    column = keys.at[lane4]
    pltpu.make_async_copy(column, column, rk).wait()

    def forward(d):
        return pltpu.make_async_remote_copy(
            column,
            keys.at[lane4],
            sk4.at[d - 1],
            rk4.at[d - 1],
            device_id={"patch": peer_at(0, (lane4 + d) % 4)},
            device_id_type=MESH,
        )

    for d in range(1, 4):
        forward(d).start()

    for copy in loads[4:]:
        copy.wait()
    tap, lane = iota((TAPS, 128), 0), iota((TAPS, 128), 1)
    for b in range(BASIS):
        both[2 * b : 2 * b + 2, 0:TAPS] = basis[b].astype(jnp.float32)
    taps_in = bf16(both[0 : 2 * BASIS, 0:TAPS])
    cbase = exact_dot(taps_in, one_hot((TAPS // 2 - tap + 128) % 128 == lane))
    rbase = [exact_dot(taps_in, one_hot(tap + 1 + 64 * odd == lane)) for odd in range(2)]
    near = jnp.abs(iota((128, 128), 0) - iota((128, 128), 1)) <= TAPS // 2
    for b in range(BASIS):
        taps = jnp.broadcast_to(cbase[2 * b : 2 * b + 1], (128, 128))
        cyclic = pltpu.roll(taps, 0, 1, stride=1, stride_axis=0)
        span = slice(b * 128, (b + 1) * 128)
        ctable[0:128, span] = bf16(jnp.where(near, cyclic, 0.0))
        ctable[128:256, span] = bf16(jnp.where(near, 0.0, cyclic))
    ctable[:, BASIS * 128 :] = jnp.zeros((256, WIDE - BASIS * 128), jnp.bfloat16)
    was, now = iota((128, 128), 0), iota((128, 128), 1)
    inside = (was % 64 >= 16) & (was % 64 < 48)
    moved_to = was // 64 * 32 + jnp.where(
        inside, was % 64 - 16, 64 + jnp.where(was % 64 < 16, was % 64, was % 64 - 32)
    )
    regroup = one_hot(moved_to == now)
    for pair in range(PAIRS):
        taps = rbase[0][4 * pair + 1 : 4 * pair + 2]
        if 2 * pair + 1 < BASIS:
            taps = taps + rbase[1][4 * pair + 3 : 4 * pair + 4]
        taps = jnp.broadcast_to(taps, (ROWS, 128))
        shifted = bf16(pltpu.roll(taps, 0, 1, stride=1, stride_axis=0))
        rtable[:, pair * 128 : (pair + 1) * 128] = exact_dot(shifted, regroup)
    column_basis = iota((BASIS, DEPTH), 1) // 128 * 2 + iota((BASIS, DEPTH), 1) % 64 // 32
    widen = one_hot(iota((BASIS, DEPTH), 0) == column_basis)
    for visit in range(VISITS):
        for term in range(3):
            coefs[visit * 8 + term : visit * 8 + term + 1, 0:BASIS] = spatial[visit, term]
    plain = coefs[:, 0:BASIS]
    plain = jnp.where(iota(plain.shape, 0) % 8 < 3, plain, 0.0)
    top = bf16(plain)
    rest = plain - top.astype(jnp.float32)
    middle = bf16(rest)
    bottom = bf16(rest - middle.astype(jnp.float32))
    coefs[...] = exact_dot(top, widen) + exact_dot(middle, widen) + exact_dot(bottom, widen)
    num[...] = jnp.zeros_like(num)
    den[...] = jnp.zeros_like(den)

    for d in range(1, 4):
        forward(d).wait_recv()

    def partner(i):
        half = (i + 1) // 2
        return n // 2 + half * (1 - 2 * (i % 2))

    side = me // 2 % 2
    owned = ((1 - core) * side + core * (2 + (side + height) % 2), 4 + side)

    def arrange(slot):
        turn_no = owned[slot]
        visit = 2 * (turn_no % 3) + height // 8
        table = keys[...].reshape(64, 128)
        patch_of = jnp.floor(table * (1.0 / 16.0))
        block_of = table - 16.0 * patch_of
        spread = one_hot(iota((128, 128), 0) == iota((128, 128), 1) % 16 + 16 * visit)
        source = iota((64, 128), 0) % 16 % 2 * 4 + iota((64, 128), 0) // 16
        held = source == iota((64, 128), 1) // 16
        gather = one_hot(iota((8, 64), 1) % 16 // 2 == iota((8, 64), 0))
        patch_of = jnp.where(held, exact_dot(bf16(patch_of), spread), 0.0)
        block_of = jnp.where(held, exact_dot(bf16(block_of), spread), 0.0)
        wanted = exact_dot(gather, bf16(patch_of)) * 16.0 + exact_dot(gather, bf16(block_of))
        wanted = wanted.astype(jnp.int32)
        pltpu.make_async_copy(y.at[slot], y.at[slot], r1.at[slot]).wait()
        data = y[slot].reshape(n * 16, 128)
        for part in range(4):
            place = iota((256, 128), 0) + 256 * part
            chosen = jnp.concatenate(
                [
                    one_hot(jnp.broadcast_to(wanted[k : k + 1], (256, 128)) == place)
                    for k in range(8)
                ],
                axis=1,
            )
            moved = exact_dot(chosen, data)
            z[slot, part * 16 : (part + 1) * 16] = bf16(moved.reshape(16, 2, 8, 128))

    def hand_out(slot):
        turn_no = owned[slot]

        def send_blocks(i, carry):
            peer = (me + partner(i)) % n
            pltpu.make_async_remote_copy(
                z.at[slot, peer],
                g.at[turn_no * 16 + height],
                s2.at[slot],
                r2.at[turn_no],
                device_id={"patch": peer},
                device_id_type=MESH,
            ).start()
            return carry

        lax.fori_loop(0, n - 1, send_blocks, 0)
        pltpu.make_async_copy(z.at[slot, me], g.at[turn_no * 16 + height], r2.at[turn_no]).start()

    arrange(0)

    @pl.when(owned[0] != 3)
    def _():
        hand_out(0)

    @pl.when(core == 0)
    def _():
        arrange(1)
        hand_out(1)

    def halo(visit, side):
        half, step = (1, 1) if side == 0 else (0, -1)
        return pltpu.make_async_remote_copy(
            g.at[pl.ds(visit * 8, 8), half],
            h.at[visit, side],
            sh.at[visit, side],
            rh.at[visit, side],
            device_id={"band": band + step},
            device_id_type=MESH,
        )

    first = (band * ROWS).astype(jnp.float32)
    u = (2.0 * (iota((ROWS, 1), 0).astype(jnp.float32) + first) + 1.0) / (bands * ROWS) - 1.0
    w = (2.0 * iota((1, COLS), 1).astype(jnp.float32) + 1.0) / COLS - 1.0
    above_on = jnp.broadcast_to(band, (8, 128)) > 0
    below_on = jnp.broadcast_to(band, (8, 128)) < bands - 1
    left_lane = iota((128, 256), 1) % 128 < 64

    def filter_columns(turn_no, part):
        images = []
        for k in range(2):
            visit = 2 * turn_no + k
            if part == 0:
                blocks = [
                    g[visit * 8 + r, half].astype(jnp.float32) for r in range(8) for half in range(2)
                ]
            else:
                blocks = [
                    jnp.where(on, h[visit, place, r].astype(jnp.float32), 0.0)
                    for place, on in ((0, above_on), (1, below_on))
                    for r in range(8)
                ]
            images.append(bf16(jnp.concatenate(blocks, axis=0)))
        moved = exact_dot(order[part], jnp.concatenate(images, axis=1))
        beside = jnp.where(left_lane, moved[128:256], moved[256:384])
        window = jnp.concatenate(
            [
                jnp.concatenate([half[0:128, k * 128 : (k + 1) * 128] for half in (moved, beside)], 1)
                for k in range(2)
            ],
            axis=0,
        )
        window = bf16(window)
        for pair in range(PAIRS):
            result = bf16(exact_dot(window, ctable[:, pair * 256 : (pair + 1) * 256]))
            for k in range(2):
                for odd in range(2):
                    at = pair * 128 + part * 64 + odd * 32
                    for c in range(4):
                        filtered[turn_no, k, at : at + 32, c * 128 : (c + 1) * 128] = result[
                            k * 128 + c * 32 : k * 128 + (c + 1) * 32,
                            odd * 128 : (odd + 1) * 128,
                        ]

    def mix_rows(turn_no):
        for k in range(2):
            visit = 2 * turn_no + k
            coef = coefs[pl.ds(pl.multiple_of(visit * 8, 8), 8)]
            table = rtable[...]
            steady = table * (coef[0:1] + u * coef[1:2])
            slope = table * coef[2:3]
            full = jnp.concatenate([steady, slope], axis=0)
            high = bf16(full)
            low = bf16(full - high.astype(jnp.float32))
            mixed = exact_dot(jnp.concatenate([high, low], axis=0), filtered[turn_no, k])
            mixed = mixed[0:64] + mixed[64:128]
            matched[visit] = mixed[0:ROWS] + w * mixed[ROWS:64]

    def weigh_two(turn_no):
        pixels = []
        for k in range(2):
            unit = (VISITS + 2 * turn_no + k) * 8
            pixels.append(
                jnp.concatenate(
                    [g[unit + r, half].astype(jnp.float32) for r in range(8) for half in range(2)], 0
                )
            )
        turned = exact_dot(worder[...], bf16(jnp.concatenate(pixels, axis=1)))
        top, bottom = num[...], den[...]
        for k in range(2):
            weights = jnp.concatenate(
                [turned[c * ROWS : (c + 1) * ROWS, k * 128 : (k + 1) * 128] for c in range(4)], axis=1
            )
            top += weights * matched[2 * turn_no + k]
            bottom += weights
        num[...], den[...] = top, bottom

    def arrived(turn_no):
        part = g.at[pl.ds(turn_no * 16, 16)]
        pltpu.make_async_copy(part, part, r2.at[turn_no]).wait()

    def share_edges(turn_no):
        arrived(turn_no)

        @pl.when(band < bands - 1)
        def _():
            halo(2 * turn_no, 0).start()
            halo(2 * turn_no + 1, 0).start()

        @pl.when(band > 0)
        def _():
            halo(2 * turn_no, 1).start()
            halo(2 * turn_no + 1, 1).start()

    def filter_pair(i, carry):
        turn_no = (i + 2) % 3

        @pl.when(band < bands - 1)
        def _():
            halo(2 * turn_no, 1).wait_recv()
            halo(2 * turn_no + 1, 1).wait_recv()

        @pl.when(band > 0)
        def _():
            halo(2 * turn_no, 0).wait_recv()
            halo(2 * turn_no + 1, 0).wait_recv()

        filter_columns(turn_no, 1)
        mix_rows(turn_no)
        return carry

    def weigh_pair(i, carry):
        turn_no = (i + 1) % 3
        arrived(turn_no + 3)
        weigh_two(turn_no)
        return carry

    share_edges(2)

    @pl.when(owned[0] == 3)
    def _():
        hand_out(0)

    filter_columns(2, 0)
    share_edges(0)
    share_edges(1)

    def filter_inner(turn_no, carry):
        filter_columns(turn_no, 0)
        return carry

    lax.fori_loop(0, 2, filter_inner, 0)
    lax.fori_loop(0, 3, filter_pair, 0)
    lax.fori_loop(0, 3, weigh_pair, 0)
    o_ref[...] = num[...] / den[...]

    @pl.when(band < bands - 1)
    def _():
        for visit in range(VISITS):
            halo(visit, 0).wait_send()

    @pl.when(band > 0)
    def _():
        for visit in range(VISITS):
            halo(visit, 1).wait_send()

    told = keys.at[0, pl.ds(0, zs - 1)]
    pltpu.make_async_copy(told, told, sk).wait()
    for d in range(1, 4):
        forward(d).wait_send()
    for visit in range(VISITS):
        gone = rows.at[pl.ds(0, zs - 1)]
        pltpu.make_async_copy(gone, gone, s1.at[visit]).wait()

        @pl.when(lane4 != place_of(visit, height))
        def _():
            pltpu.make_async_copy(rows.at[0], rows.at[0], s1b.at[visit]).wait()

    relayed = z.at[0, pl.ds(0, n - 1)]
    pltpu.make_async_copy(relayed, relayed, s2.at[0]).wait()

    @pl.when(core == 0)
    def _():
        pltpu.make_async_copy(relayed, relayed, s2.at[1]).wait()


def orders():
    order = np.zeros((3, 4, 64, 256), np.float32)
    for c in range(4):
        for t in range(64):
            for kind, shift in ((0, 0), (1, 1), (2, -1)):
                d = c + shift
                if not 0 <= d < 4:
                    continue
                if t < 16:
                    place = (t % 8) * 8 + (t // 8) * 4 + d
                elif t < 48:
                    s = t - 16
                    place = 64 + (s % 8) * 16 + (s // 8) * 4 + d
                else:
                    s = t - 48
                    place = 192 + (s % 8) * 8 + (s // 8) * 4 + d
                order[kind, c, t, place] = 1.0
    worder = np.zeros((4, ROWS, 128), np.float32)
    for c in range(4):
        for s in range(ROWS):
            worder[c, s, (s % 8) * 16 + (s // 8) * 4 + c] = 1.0
    inner = order[:, :, 16:48, 64:192].reshape(384, 128)
    outer = np.concatenate([order[:, :, :16], order[:, :, 48:]], axis=2)
    outer = np.concatenate([outer[..., :64], outer[..., 192:]], axis=3).reshape(384, 128)
    return np.stack([inner, outer]), worder.reshape(128, 128)


def per_device(tile_flux, tile_weight, dest_patch, dest_block, basis, spatial):
    n = lax.axis_size("patch")
    vmem, dma = pltpu.VMEM, pltpu.SemaphoreType.DMA
    order, worder = orders()
    coadd = pl.pallas_call(
        kernel,
        out_shape=vmem((ROWS, COLS), jnp.float32),
        in_specs=[pl.BlockSpec(memory_space=pl.ANY)] * 8,
        out_specs=pl.BlockSpec(memory_space=vmem),
        scratch_shapes=[
            vmem((2, VISITS, 16, 8, 128), jnp.bfloat16),
            vmem((2, VISITS, 16), jnp.int32),
            vmem((BASIS, 2, TAPS), jnp.bfloat16),
            vmem((VISITS, 3, 1, BASIS), jnp.float32),
            vmem((48, 128), jnp.float32),
            vmem((2, 384, 128), jnp.bfloat16),
            vmem((128, 128), jnp.bfloat16),
            vmem((VISITS * 16, 16, 128), jnp.bfloat16),
            vmem((1, 128), jnp.float32),
            vmem((2, n, 16, 128), jnp.bfloat16),
            vmem((4, n // 4, 1, 128), jnp.float32),
            vmem((2, n, 2, 8, 128), jnp.bfloat16),
            vmem((VISITS * 16, 2, 8, 128), jnp.bfloat16),
            vmem((VISITS, 2, 8, 8, 128), jnp.bfloat16),
            vmem((256, WIDE), jnp.bfloat16),
            vmem((ROWS, DEPTH), jnp.float32),
            vmem((VISITS * 8, DEPTH), jnp.float32),
            vmem((3, 2, DEPTH, COLS), jnp.bfloat16),
            vmem((VISITS, ROWS, COLS), jnp.float32),
            vmem((ROWS, COLS), jnp.float32),
            vmem((ROWS, COLS), jnp.float32),
            dma((8,)),
            pltpu.SemaphoreType.REGULAR((len(LEVELS),)),
            dma((VISITS,)),
            dma((VISITS,)),
            dma((2,)),
            dma,
            dma,
            dma((3,)),
            dma((3,)),
            dma((2,)),
            dma((VISITS,)),
            dma((VISITS, 2)),
            dma((VISITS, 2)),
        ],
        compiler_params=pltpu.CompilerParams(collective_id=0, has_side_effects=True),
        name="coadd",
    )(
        tile_flux,
        tile_weight,
        dest_patch,
        dest_block,
        basis.transpose(1, 0, 2),
        spatial.transpose(1, 2, 0, 3),
        jnp.asarray(order, jnp.bfloat16),
        jnp.asarray(worder, jnp.bfloat16),
    )
    return coadd[None]


def solution(mesh):
    in_specs = (
        P(None, ("patch", "band"), None, None),
        P(None, ("patch", "band"), None, None),
        P(None, ("patch", "band")),
        P(None, ("patch", "band")),
        P(),
        P("patch", None, None, None),
    )
    out_specs = P("patch", "band", None)
    return jax.shard_map(
        per_device, mesh=mesh, in_specs=in_specs, out_specs=out_specs, check_vma=False
    )
```

```python
import jax
import jax.numpy as jnp
import numpy as np
from jax import lax
from jax.experimental import pallas as pl
from jax.experimental.pallas import tpu as pltpu
from jax.sharding import PartitionSpec as P

MESH = pl.DeviceIdType.MESH
VISITS = 6
BASIS = 21
TAPS = 31
ROWS = 32
COLS = 512
NEAR = 4
AHEAD = 3
ROUNDS = 6
P1ORDER = (0, 1, 2, 4, 5, 3)
LEVELS = ((4, 0), (0, ROUNDS))
PAIRS = (BASIS + 1) // 2
DEPTH = PAIRS * 128
WIDE = PAIRS * 256


def bf16(value):
    return value.astype(jnp.bfloat16)


def iota(shape, dim):
    return lax.broadcasted_iota(jnp.int32, shape, dim)


def exact_dot(a, b):
    return jnp.dot(a, b, preferred_element_type=jnp.float32)


def one_hot(condition):
    return bf16(jnp.where(condition, 1.0, 0.0))


def kernel(flux_hbm, weight_hbm, patch_hbm, block_hbm, basis_hbm, spatial_hbm, order_hbm, worder_hbm,
           o_ref, tiles, dest, basis, spatial, both, order, worder, rows, key_row, y, keys, z, g, h,
           ctable, rtable, coefs, blend, filtered, matched, num, den,
           load, heard, s1, s1b, r1, sk, rk, sk4, rk4, s2, r2, sh, rh):
    n, bands = lax.axis_size("patch"), lax.axis_size("band")
    me, band = lax.axis_index("patch"), lax.axis_index("band")
    core = me % 2

    zs = n // 4
    height, lane4 = me // 4, me % 4

    def peer_at(step, place):
        return ((height + step + zs) % zs) * 4 + place

    barrier = pltpu.get_barrier_semaphore()

    def greet(i, carry):
        peer = peer_at(i // 4 - NEAR, i % 4)
        pl.semaphore_signal(barrier, inc=1, device_id={"patch": peer}, device_id_type=MESH)
        return carry

    lax.fori_loop(0, NEAR * 4, greet, 0)
    lax.fori_loop(NEAR * 4 + 4, NEAR * 8 + 4, greet, 0)
    for d in range(1, 4):
        peer = peer_at(0, (lane4 + d) % 4)
        pl.semaphore_signal(barrier, inc=1, device_id={"patch": peer}, device_id_type=MESH)

    @pl.when(band > 0)
    def _():
        pl.semaphore_signal(barrier, inc=1, device_id={"band": band - 1}, device_id_type=MESH)

    @pl.when(band < bands - 1)
    def _():
        pl.semaphore_signal(barrier, inc=1, device_id={"band": band + 1}, device_id_type=MESH)

    loads = [
        pltpu.make_async_copy(source, target, load.at[i])
        for i, (source, target) in enumerate(
            (
                (patch_hbm, dest.at[0]),
                (block_hbm, dest.at[1]),
                (flux_hbm, tiles.at[0]),
                (weight_hbm, tiles.at[1]),
                (basis_hbm, basis),
                (spatial_hbm, spatial),
                (order_hbm, order),
                (worder_hbm, worder),
            )
        )
    ]
    for copy in loads:
        copy.start()

    loads[0].wait()
    loads[1].wait()
    spread = one_hot(iota((16, 128), 0) == iota((16, 128), 1) % 16)
    patch_lane = exact_dot(bf16(dest[0].astype(jnp.float32)), spread)
    block_lane = exact_dot(bf16(dest[1].astype(jnp.float32)), spread)
    key_lane = patch_lane * 16.0 + block_lane
    key_lane = jnp.where(iota((VISITS, 128), 0) == iota((VISITS, 128), 1) // 16, key_lane, 0.0)
    key_row[...] = jnp.sum(key_lane, axis=0, keepdims=True)
    turn = one_hot(
        (iota((128, 128), 0) % 16) * 8 + iota((128, 128), 0) // 16 == iota((128, 128), 1)
    )
    loads[2].wait()
    loads[3].wait()

    def turn_rows(visit, carry):
        for kind in range(2):
            pixels = bf16(
                jnp.concatenate(
                    [tiles[kind, visit, t].astype(jnp.float32) for t in range(16)], axis=0
                )
            )
            turned = bf16(exact_dot(turn, pixels))
            for r in range(8):
                rows[kind * VISITS * 8 + visit * 8 + r] = turned[r * 16 : (r + 1) * 16]
        return carry

    lax.fori_loop(0, VISITS, turn_rows, 0)

    pl.semaphore_wait(
        barrier, NEAR * 8 + 3 + (band + bands - 1) // bands + (2 * bands - 2 - band) // bands
    )

    def send_key(step):
        pltpu.make_async_remote_copy(
            key_row,
            keys.at[lane4, height],
            sk,
            rk,
            device_id={"patch": peer_at(step, lane4)},
            device_id_type=MESH,
        ).start()

    def place_of(turn_no, at):
        if turn_no in (2, 3):
            return (at + turn_no) % 2 * 2 + 1
        return turn_no % 2 * 2

    def send_row(turn_no, step):
        place = place_of(turn_no, height + step + zs)
        pltpu.make_async_remote_copy(
            rows.at[turn_no * 16 + (height + step + zs) % zs],
            y.at[turn_no // 4, me],
            s1.at[turn_no],
            r1.at[turn_no // 4],
            device_id={"patch": peer_at(step, place)},
            device_id_type=MESH,
        ).start()

    def send_ring(inner, outer, rounds, with_keys):
        def one(i, carry):
            reach = outer - i
            for step in (reach, -reach):
                if with_keys:
                    send_key(step)
                for turn_no in rounds:
                    send_row(turn_no, step)
            return carry

        lax.fori_loop(0, outer - inner, one, 0)
        if outer == zs // 2 - 1:
            if with_keys:
                send_key(zs // 2)
            for turn_no in rounds:
                send_row(turn_no, zs // 2)

    pltpu.make_async_copy(key_row, keys.at[lane4, height], rk).start()

    def own_height(rounds):
        for turn_no in rounds:
            place = place_of(turn_no, height)

            @pl.when(lane4 == place)
            def _():
                pltpu.make_async_copy(
                    rows.at[turn_no * 16 + height], y.at[turn_no // 4, me], r1.at[turn_no // 4]
                ).start()

            @pl.when(lane4 != place)
            def _():
                pltpu.make_async_remote_copy(
                    rows.at[turn_no * 16 + height],
                    y.at[turn_no // 4, me],
                    s1b.at[turn_no],
                    r1.at[turn_no // 4],
                    device_id={"patch": peer_at(0, place)},
                    device_id_type=MESH,
                ).start()

    known, sent = NEAR, [0] * ROUNDS
    for level, (reach, count) in enumerate(LEVELS):
        if reach:
            for step in (reach, -reach):
                pl.semaphore_signal(
                    heard.at[level],
                    inc=1,
                    device_id={"patch": peer_at(step, lane4)},
                    device_id_type=MESH,
                )
        if level == 0:
            send_ring(0, known, (0,), True)
            if AHEAD > 1:
                send_ring(0, known, tuple(range(1, AHEAD)), False)
            own_height(range(ROUNDS))
            sent = [known] * AHEAD + [0] * (ROUNDS - AHEAD)
        else:
            for turn_no in P1ORDER[:count]:
                send_ring(sent[turn_no], known, (turn_no,), sent[turn_no] == before and turn_no == 0)
                sent[turn_no] = known
        before = known
        if reach:
            pl.semaphore_wait(heard.at[level], 2)
            known = min(known + reach, zs // 2 - 1)

    column = keys.at[lane4]
    pltpu.make_async_copy(column, column, rk).wait()

    def forward(d):
        return pltpu.make_async_remote_copy(
            column,
            keys.at[lane4],
            sk4.at[d - 1],
            rk4.at[d - 1],
            device_id={"patch": peer_at(0, (lane4 + d) % 4)},
            device_id_type=MESH,
        )

    for d in range(1, 4):
        forward(d).start()

    for copy in loads[4:]:
        copy.wait()
    tap, lane = iota((TAPS, 128), 0), iota((TAPS, 128), 1)
    for b in range(BASIS):
        both[2 * b : 2 * b + 2, 0:TAPS] = basis[b].astype(jnp.float32)
    taps_in = bf16(both[0 : 2 * BASIS, 0:TAPS])
    cbase = exact_dot(taps_in, one_hot((TAPS // 2 - tap + 128) % 128 == lane))
    rbase = [exact_dot(taps_in, one_hot(tap + 1 + 64 * odd == lane)) for odd in range(2)]
    near = jnp.abs(iota((128, 128), 0) - iota((128, 128), 1)) <= TAPS // 2
    for b in range(BASIS):
        taps = jnp.broadcast_to(cbase[2 * b : 2 * b + 1], (128, 128))
        cyclic = pltpu.roll(taps, 0, 1, stride=1, stride_axis=0)
        span = slice(b * 128, (b + 1) * 128)
        ctable[0:128, span] = bf16(jnp.where(near, cyclic, 0.0))
        ctable[128:256, span] = bf16(jnp.where(near, 0.0, cyclic))
    ctable[:, BASIS * 128 :] = jnp.zeros((256, WIDE - BASIS * 128), jnp.bfloat16)
    was, now = iota((128, 128), 0), iota((128, 128), 1)
    inside = (was % 64 >= 16) & (was % 64 < 48)
    moved_to = was // 64 * 32 + jnp.where(
        inside, was % 64 - 16, 64 + jnp.where(was % 64 < 16, was % 64, was % 64 - 32)
    )
    regroup = one_hot(moved_to == now)
    for pair in range(PAIRS):
        taps = rbase[0][4 * pair + 1 : 4 * pair + 2]
        if 2 * pair + 1 < BASIS:
            taps = taps + rbase[1][4 * pair + 3 : 4 * pair + 4]
        taps = jnp.broadcast_to(taps, (ROWS, 128))
        shifted = bf16(pltpu.roll(taps, 0, 1, stride=1, stride_axis=0))
        rtable[:, pair * 128 : (pair + 1) * 128] = exact_dot(shifted, regroup)
    column_basis = iota((BASIS, DEPTH), 1) // 128 * 2 + iota((BASIS, DEPTH), 1) % 64 // 32
    widen = one_hot(iota((BASIS, DEPTH), 0) == column_basis)
    for visit in range(VISITS):
        for term in range(3):
            coefs[visit * 8 + term : visit * 8 + term + 1, 0:BASIS] = spatial[visit, term]
    plain = coefs[:, 0:BASIS]
    plain = jnp.where(iota(plain.shape, 0) % 8 < 3, plain, 0.0)
    top = bf16(plain)
    rest = plain - top.astype(jnp.float32)
    middle = bf16(rest)
    bottom = bf16(rest - middle.astype(jnp.float32))
    coefs[...] = exact_dot(top, widen) + exact_dot(middle, widen) + exact_dot(bottom, widen)
    first = (band * ROWS).astype(jnp.float32)
    u = (2.0 * (iota((ROWS, 1), 0).astype(jnp.float32) + first) + 1.0) / (bands * ROWS) - 1.0

    def fill_blend(visit, carry):
        coef = coefs[pl.ds(pl.multiple_of(visit * 8, 8), 8)]
        table = rtable[...]
        steady = table * (coef[0:1] + u * coef[1:2])
        slope = table * coef[2:3]
        full = jnp.concatenate([steady, slope], axis=0)
        high = bf16(full)
        low = bf16(full - high.astype(jnp.float32))
        blend[visit] = jnp.concatenate([high, low], axis=0)
        return carry

    lax.fori_loop(0, VISITS, fill_blend, 0)
    num[...] = jnp.zeros_like(num)
    den[...] = jnp.zeros_like(den)

    for d in range(1, 4):
        forward(d).wait_recv()

    def partner(i):
        half = (i + 1) // 2
        return n // 2 + half * (1 - 2 * (i % 2))

    side = me // 2 % 2
    owned = ((1 - core) * side + core * (2 + (side + height) % 2), 4 + side)

    def arrange(slot):
        turn_no = owned[slot]
        visit = 2 * (turn_no % 3) + height // 8
        table = keys[...].reshape(64, 128)
        patch_of = jnp.floor(table * (1.0 / 16.0))
        block_of = table - 16.0 * patch_of
        spread = one_hot(iota((128, 128), 0) == iota((128, 128), 1) % 16 + 16 * visit)
        source = iota((64, 128), 0) % 16 % 2 * 4 + iota((64, 128), 0) // 16
        held = source == iota((64, 128), 1) // 16
        gather = one_hot(iota((8, 64), 1) % 16 // 2 == iota((8, 64), 0))
        patch_of = jnp.where(held, exact_dot(bf16(patch_of), spread), 0.0)
        block_of = jnp.where(held, exact_dot(bf16(block_of), spread), 0.0)
        wanted = exact_dot(gather, bf16(patch_of)) * 16.0 + exact_dot(gather, bf16(block_of))
        wanted = wanted.astype(jnp.int32)
        pltpu.make_async_copy(y.at[slot], y.at[slot], r1.at[slot]).wait()
        data = y[slot].reshape(n * 16, 128)
        for part in range(4):
            place = iota((256, 128), 0) + 256 * part
            chosen = jnp.concatenate(
                [
                    one_hot(jnp.broadcast_to(wanted[k : k + 1], (256, 128)) == place)
                    for k in range(8)
                ],
                axis=1,
            )
            moved = exact_dot(chosen, data)
            z[slot, part * 16 : (part + 1) * 16] = bf16(moved.reshape(16, 2, 8, 128))

    def hand_out(slot):
        turn_no = owned[slot]

        def send_blocks(i, carry):
            peer = (me + partner(i)) % n
            pltpu.make_async_remote_copy(
                z.at[slot, peer],
                g.at[turn_no * 16 + height],
                s2.at[slot],
                r2.at[turn_no],
                device_id={"patch": peer},
                device_id_type=MESH,
            ).start()
            return carry

        lax.fori_loop(0, n - 1, send_blocks, 0)
        pltpu.make_async_copy(z.at[slot, me], g.at[turn_no * 16 + height], r2.at[turn_no]).start()

    arrange(0)

    @pl.when(owned[0] != 3)
    def _():
        hand_out(0)

    @pl.when(core == 0)
    def _():
        arrange(1)
        hand_out(1)

    def halo(turn_no, side):
        half, step = (1, 1) if side == 0 else (0, -1)
        return pltpu.make_async_remote_copy(
            g.at[pl.ds(turn_no * 16, 16), half],
            h.at[turn_no, side],
            sh.at[turn_no, side],
            rh.at[turn_no, side],
            device_id={"band": band + step},
            device_id_type=MESH,
        )

    w = (2.0 * iota((1, COLS), 1).astype(jnp.float32) + 1.0) / COLS - 1.0
    above_on = jnp.broadcast_to(band, (8, 128)) > 0
    below_on = jnp.broadcast_to(band, (8, 128)) < bands - 1
    left_lane = iota((128, 256), 1) % 128 < 64

    def filter_columns(turn_no, part):
        images = []
        for k in range(2):
            visit = 2 * turn_no + k
            if part == 0:
                blocks = [
                    g[visit * 8 + r, half].astype(jnp.float32) for r in range(8) for half in range(2)
                ]
            else:
                blocks = [
                    jnp.where(on, h[turn_no, place, k * 8 + r].astype(jnp.float32), 0.0)
                    for place, on in ((0, above_on), (1, below_on))
                    for r in range(8)
                ]
            images.append(bf16(jnp.concatenate(blocks, axis=0)))
        moved = exact_dot(order[part], jnp.concatenate(images, axis=1))
        beside = jnp.where(left_lane, moved[128:256], moved[256:384])
        window = jnp.concatenate(
            [
                jnp.concatenate([half[0:128, k * 128 : (k + 1) * 128] for half in (moved, beside)], 1)
                for k in range(2)
            ],
            axis=0,
        )
        window = bf16(window)
        for pair in range(PAIRS):
            result = bf16(exact_dot(window, ctable[:, pair * 256 : (pair + 1) * 256]))
            for k in range(2):
                for odd in range(2):
                    at = pair * 128 + part * 64 + odd * 32
                    for c in range(4):
                        filtered[turn_no, k, at : at + 32, c * 128 : (c + 1) * 128] = result[
                            k * 128 + c * 32 : k * 128 + (c + 1) * 32,
                            odd * 128 : (odd + 1) * 128,
                        ]

    def mix_rows(turn_no):
        for k in range(2):
            visit = 2 * turn_no + k
            mixed = exact_dot(blend[visit], filtered[turn_no, k])
            mixed = mixed[0:64] + mixed[64:128]
            matched[visit] = mixed[0:ROWS] + w * mixed[ROWS:64]

    def weigh_two(turn_no):
        pixels = []
        for k in range(2):
            unit = (VISITS + 2 * turn_no + k) * 8
            pixels.append(
                jnp.concatenate(
                    [g[unit + r, half].astype(jnp.float32) for r in range(8) for half in range(2)], 0
                )
            )
        turned = exact_dot(worder[...], bf16(jnp.concatenate(pixels, axis=1)))
        top, bottom = num[...], den[...]
        for k in range(2):
            weights = jnp.concatenate(
                [turned[c * ROWS : (c + 1) * ROWS, k * 128 : (k + 1) * 128] for c in range(4)], axis=1
            )
            top += weights * matched[2 * turn_no + k]
            bottom += weights
        num[...], den[...] = top, bottom

    def arrived(turn_no):
        part = g.at[pl.ds(turn_no * 16, 16)]
        pltpu.make_async_copy(part, part, r2.at[turn_no]).wait()

    def share_edges(turn_no):
        arrived(turn_no)

        @pl.when(band < bands - 1)
        def _():
            halo(turn_no, 0).start()

        @pl.when(band > 0)
        def _():
            halo(turn_no, 1).start()

    def filter_pair(i, carry):
        turn_no = (i + 2) % 3

        @pl.when(band < bands - 1)
        def _():
            halo(turn_no, 1).wait_recv()

        @pl.when(band > 0)
        def _():
            halo(turn_no, 0).wait_recv()

        filter_columns(turn_no, 1)
        mix_rows(turn_no)
        return carry

    def weigh_pair(i, carry):
        turn_no = (i + 1) % 3
        arrived(turn_no + 3)
        weigh_two(turn_no)
        return carry

    share_edges(2)

    @pl.when(owned[0] == 3)
    def _():
        hand_out(0)

    filter_columns(2, 0)
    share_edges(0)
    share_edges(1)

    def filter_inner(turn_no, carry):
        filter_columns(turn_no, 0)
        return carry

    lax.fori_loop(0, 2, filter_inner, 0)
    lax.fori_loop(0, 3, filter_pair, 0)
    lax.fori_loop(0, 3, weigh_pair, 0)
    o_ref[...] = num[...] / den[...]

    @pl.when(band < bands - 1)
    def _():
        for turn_no in range(3):
            halo(turn_no, 0).wait_send()

    @pl.when(band > 0)
    def _():
        for turn_no in range(3):
            halo(turn_no, 1).wait_send()

    told = keys.at[0, pl.ds(0, zs - 1)]
    pltpu.make_async_copy(told, told, sk).wait()
    for d in range(1, 4):
        forward(d).wait_send()
    for visit in range(VISITS):
        gone = rows.at[pl.ds(0, zs - 1)]
        pltpu.make_async_copy(gone, gone, s1.at[visit]).wait()

        @pl.when(lane4 != place_of(visit, height))
        def _():
            pltpu.make_async_copy(rows.at[0], rows.at[0], s1b.at[visit]).wait()

    relayed = z.at[0, pl.ds(0, n - 1)]
    pltpu.make_async_copy(relayed, relayed, s2.at[0]).wait()

    @pl.when(core == 0)
    def _():
        pltpu.make_async_copy(relayed, relayed, s2.at[1]).wait()


def orders():
    order = np.zeros((3, 4, 64, 256), np.float32)
    for c in range(4):
        for t in range(64):
            for kind, shift in ((0, 0), (1, 1), (2, -1)):
                d = c + shift
                if not 0 <= d < 4:
                    continue
                if t < 16:
                    place = (t % 8) * 8 + (t // 8) * 4 + d
                elif t < 48:
                    s = t - 16
                    place = 64 + (s % 8) * 16 + (s // 8) * 4 + d
                else:
                    s = t - 48
                    place = 192 + (s % 8) * 8 + (s // 8) * 4 + d
                order[kind, c, t, place] = 1.0
    worder = np.zeros((4, ROWS, 128), np.float32)
    for c in range(4):
        for s in range(ROWS):
            worder[c, s, (s % 8) * 16 + (s // 8) * 4 + c] = 1.0
    inner = order[:, :, 16:48, 64:192].reshape(384, 128)
    outer = np.concatenate([order[:, :, :16], order[:, :, 48:]], axis=2)
    outer = np.concatenate([outer[..., :64], outer[..., 192:]], axis=3).reshape(384, 128)
    return np.stack([inner, outer]), worder.reshape(128, 128)


def per_device(tile_flux, tile_weight, dest_patch, dest_block, basis, spatial):
    n = lax.axis_size("patch")
    vmem, dma = pltpu.VMEM, pltpu.SemaphoreType.DMA
    order, worder = orders()
    coadd = pl.pallas_call(
        kernel,
        out_shape=vmem((ROWS, COLS), jnp.float32),
        in_specs=[pl.BlockSpec(memory_space=pl.ANY)] * 8,
        out_specs=pl.BlockSpec(memory_space=vmem),
        scratch_shapes=[
            vmem((2, VISITS, 16, 8, 128), jnp.bfloat16),
            vmem((2, VISITS, 16), jnp.int32),
            vmem((BASIS, 2, TAPS), jnp.bfloat16),
            vmem((VISITS, 3, 1, BASIS), jnp.float32),
            vmem((48, 128), jnp.float32),
            vmem((2, 384, 128), jnp.bfloat16),
            vmem((128, 128), jnp.bfloat16),
            vmem((VISITS * 16, 16, 128), jnp.bfloat16),
            vmem((1, 128), jnp.float32),
            vmem((2, n, 16, 128), jnp.bfloat16),
            vmem((4, n // 4, 1, 128), jnp.float32),
            vmem((2, n, 2, 8, 128), jnp.bfloat16),
            vmem((VISITS * 16, 2, 8, 128), jnp.bfloat16),
            vmem((3, 2, 16, 8, 128), jnp.bfloat16),
            vmem((256, WIDE), jnp.bfloat16),
            vmem((ROWS, DEPTH), jnp.float32),
            vmem((VISITS * 8, DEPTH), jnp.float32),
            vmem((VISITS, 4 * ROWS, DEPTH), jnp.bfloat16),
            vmem((3, 2, DEPTH, COLS), jnp.bfloat16),
            vmem((VISITS, ROWS, COLS), jnp.float32),
            vmem((ROWS, COLS), jnp.float32),
            vmem((ROWS, COLS), jnp.float32),
            dma((8,)),
            pltpu.SemaphoreType.REGULAR((len(LEVELS),)),
            dma((VISITS,)),
            dma((VISITS,)),
            dma((2,)),
            dma,
            dma,
            dma((3,)),
            dma((3,)),
            dma((2,)),
            dma((VISITS,)),
            dma((3, 2)),
            dma((3, 2)),
        ],
        compiler_params=pltpu.CompilerParams(collective_id=0, has_side_effects=True),
        name="coadd",
    )(
        tile_flux,
        tile_weight,
        dest_patch,
        dest_block,
        basis.transpose(1, 0, 2),
        spatial.transpose(1, 2, 0, 3),
        jnp.asarray(order, jnp.bfloat16),
        jnp.asarray(worder, jnp.bfloat16),
    )
    return coadd[None]


def solution(mesh):
    in_specs = (
        P(None, ("patch", "band"), None, None),
        P(None, ("patch", "band"), None, None),
        P(None, ("patch", "band")),
        P(None, ("patch", "band")),
        P(),
        P("patch", None, None, None),
    )
    out_specs = P("patch", "band", None)
    return jax.shard_map(
        per_device, mesh=mesh, in_specs=in_specs, out_specs=out_specs, check_vma=False
    )
```

```python
import jax
import jax.numpy as jnp
import numpy as np
from jax import lax
from jax.experimental import pallas as pl
from jax.experimental.pallas import tpu as pltpu
from jax.sharding import PartitionSpec as P

MESH = pl.DeviceIdType.MESH
VISITS = 6
BASIS = 21
TAPS = 31
ROWS = 32
COLS = 512
NEAR = 4
AHEAD = 3
ROUNDS = 6
P1ORDER = (0, 1, 2, 4, 5, 3)
LEVELS = ((4, 0), (0, ROUNDS))
PAIRS = (BASIS + 1) // 2
DEPTH = PAIRS * 128
WIDE = PAIRS * 256


def bf16(value):
    return value.astype(jnp.bfloat16)


def iota(shape, dim):
    return lax.broadcasted_iota(jnp.int32, shape, dim)


def exact_dot(a, b):
    return jnp.dot(a, b, preferred_element_type=jnp.float32)


def one_hot(condition):
    return bf16(jnp.where(condition, 1.0, 0.0))


def kernel(flux_hbm, weight_hbm, patch_hbm, block_hbm, basis_hbm, spatial_hbm, order_hbm, worder_hbm,
           o_ref, tiles, dest, basis, spatial, both, order, worder, rows, key_row, y, keys, z, g, h,
           ctable, rtable, coefs, blend, filtered, matched, num, den,
           load, heard, s1, s1b, r1, sk, rk, sk4, rk4, s2, r2, sh, rh):
    n, bands = lax.axis_size("patch"), lax.axis_size("band")
    me, band = lax.axis_index("patch"), lax.axis_index("band")
    core = me % 2

    zs = n // 4
    height, lane4 = me // 4, me % 4

    def peer_at(step, place):
        return ((height + step + zs) % zs) * 4 + place

    barrier = pltpu.get_barrier_semaphore()

    def greet(i, carry):
        peer = peer_at(i // 4 - NEAR, i % 4)
        pl.semaphore_signal(barrier, inc=1, device_id={"patch": peer}, device_id_type=MESH)
        return carry

    lax.fori_loop(0, NEAR * 4, greet, 0)
    lax.fori_loop(NEAR * 4 + 4, NEAR * 8 + 4, greet, 0)
    for d in range(1, 4):
        peer = peer_at(0, (lane4 + d) % 4)
        pl.semaphore_signal(barrier, inc=1, device_id={"patch": peer}, device_id_type=MESH)

    @pl.when(band > 0)
    def _():
        pl.semaphore_signal(barrier, inc=1, device_id={"band": band - 1}, device_id_type=MESH)

    @pl.when(band < bands - 1)
    def _():
        pl.semaphore_signal(barrier, inc=1, device_id={"band": band + 1}, device_id_type=MESH)

    loads = [
        pltpu.make_async_copy(source, target, load.at[i])
        for i, (source, target) in enumerate(
            (
                (patch_hbm, dest.at[0]),
                (block_hbm, dest.at[1]),
                (flux_hbm, tiles.at[0]),
                (weight_hbm, tiles.at[1]),
                (basis_hbm, basis),
                (spatial_hbm, spatial),
                (order_hbm, order),
                (worder_hbm, worder),
            )
        )
    ]
    for copy in loads:
        copy.start()

    loads[0].wait()
    loads[1].wait()
    spread = one_hot(iota((16, 128), 0) == iota((16, 128), 1) % 16)
    patch_lane = exact_dot(bf16(dest[0].astype(jnp.float32)), spread)
    block_lane = exact_dot(bf16(dest[1].astype(jnp.float32)), spread)
    key_lane = patch_lane * 16.0 + block_lane
    key_lane = jnp.where(iota((VISITS, 128), 0) == iota((VISITS, 128), 1) // 16, key_lane, 0.0)
    key_row[...] = jnp.sum(key_lane, axis=0, keepdims=True)
    turn = one_hot(
        (iota((128, 128), 0) % 16) * 8 + iota((128, 128), 0) // 16 == iota((128, 128), 1)
    )
    loads[2].wait()
    loads[3].wait()

    def turn_rows(visit, carry):
        for kind in range(2):
            pixels = bf16(
                jnp.concatenate(
                    [tiles[kind, visit, t].astype(jnp.float32) for t in range(16)], axis=0
                )
            )
            turned = bf16(exact_dot(turn, pixels))
            for r in range(8):
                rows[kind * VISITS * 8 + visit * 8 + r] = turned[r * 16 : (r + 1) * 16]
        return carry

    lax.fori_loop(0, VISITS, turn_rows, 0)

    pl.semaphore_wait(
        barrier, NEAR * 8 + 3 + (band + bands - 1) // bands + (2 * bands - 2 - band) // bands
    )

    def send_key(step):
        pltpu.make_async_remote_copy(
            key_row,
            keys.at[lane4, height],
            sk,
            rk,
            device_id={"patch": peer_at(step, lane4)},
            device_id_type=MESH,
        ).start()

    def place_of(turn_no, at):
        if turn_no in (2, 3):
            return (at + turn_no) % 2 * 2 + 1
        return turn_no % 2 * 2

    def send_row(turn_no, step):
        place = place_of(turn_no, height + step + zs)
        pltpu.make_async_remote_copy(
            rows.at[turn_no * 16 + (height + step + zs) % zs],
            y.at[turn_no // 4, me],
            s1.at[turn_no],
            r1.at[turn_no // 4],
            device_id={"patch": peer_at(step, place)},
            device_id_type=MESH,
        ).start()

    def send_ring(inner, outer, rounds, with_keys):
        def one(i, carry):
            reach = outer - i
            for step in (reach, -reach):
                if with_keys:
                    send_key(step)
                for turn_no in rounds:
                    send_row(turn_no, step)
            return carry

        lax.fori_loop(0, outer - inner, one, 0)
        if outer == zs // 2 - 1:
            if with_keys:
                send_key(zs // 2)
            for turn_no in rounds:
                send_row(turn_no, zs // 2)

    pltpu.make_async_copy(key_row, keys.at[lane4, height], rk).start()

    def own_height(rounds):
        for turn_no in rounds:
            place = place_of(turn_no, height)

            @pl.when(lane4 == place)
            def _():
                pltpu.make_async_copy(
                    rows.at[turn_no * 16 + height], y.at[turn_no // 4, me], r1.at[turn_no // 4]
                ).start()

            @pl.when(lane4 != place)
            def _():
                pltpu.make_async_remote_copy(
                    rows.at[turn_no * 16 + height],
                    y.at[turn_no // 4, me],
                    s1b.at[turn_no],
                    r1.at[turn_no // 4],
                    device_id={"patch": peer_at(0, place)},
                    device_id_type=MESH,
                ).start()

    known, sent = NEAR, [0] * ROUNDS
    for level, (reach, count) in enumerate(LEVELS):
        if reach:
            for step in (reach, -reach):
                pl.semaphore_signal(
                    heard.at[level],
                    inc=1,
                    device_id={"patch": peer_at(step, lane4)},
                    device_id_type=MESH,
                )
        if level == 0:
            send_ring(0, known, (0,), True)
            if AHEAD > 1:
                send_ring(0, known, tuple(range(1, AHEAD)), False)
            own_height(range(ROUNDS))
            sent = [known] * AHEAD + [0] * (ROUNDS - AHEAD)
        else:
            for turn_no in P1ORDER[:count]:
                send_ring(sent[turn_no], known, (turn_no,), sent[turn_no] == before and turn_no == 0)
                sent[turn_no] = known
        before = known
        if reach:
            pl.semaphore_wait(heard.at[level], 2)
            known = min(known + reach, zs // 2 - 1)

    column = keys.at[lane4]
    pltpu.make_async_copy(column, column, rk).wait()

    def forward(d):
        return pltpu.make_async_remote_copy(
            column,
            keys.at[lane4],
            sk4.at[d - 1],
            rk4.at[d - 1],
            device_id={"patch": peer_at(0, (lane4 + d) % 4)},
            device_id_type=MESH,
        )

    for d in range(1, 4):
        forward(d).start()

    for copy in loads[4:]:
        copy.wait()
    tap, lane = iota((TAPS, 128), 0), iota((TAPS, 128), 1)
    for b in range(BASIS):
        both[2 * b : 2 * b + 2, 0:TAPS] = basis[b].astype(jnp.float32)
    taps_in = bf16(both[0 : 2 * BASIS, 0:TAPS])
    cbase = exact_dot(taps_in, one_hot((TAPS // 2 - tap + 128) % 128 == lane))
    rbase = [exact_dot(taps_in, one_hot(tap + 1 + 64 * odd == lane)) for odd in range(2)]
    near = jnp.abs(iota((128, 128), 0) - iota((128, 128), 1)) <= TAPS // 2
    for b in range(BASIS):
        taps = jnp.broadcast_to(cbase[2 * b : 2 * b + 1], (128, 128))
        cyclic = pltpu.roll(taps, 0, 1, stride=1, stride_axis=0)
        span = slice(b * 128, (b + 1) * 128)
        ctable[0:128, span] = bf16(jnp.where(near, cyclic, 0.0))
        ctable[128:256, span] = bf16(jnp.where(near, 0.0, cyclic))
    ctable[:, BASIS * 128 :] = jnp.zeros((256, WIDE - BASIS * 128), jnp.bfloat16)
    was, now = iota((128, 128), 0), iota((128, 128), 1)
    inside = (was % 64 >= 16) & (was % 64 < 48)
    moved_to = was // 64 * 32 + jnp.where(
        inside, was % 64 - 16, 64 + jnp.where(was % 64 < 16, was % 64, was % 64 - 32)
    )
    regroup = one_hot(moved_to == now)
    for pair in range(PAIRS):
        taps = rbase[0][4 * pair + 1 : 4 * pair + 2]
        if 2 * pair + 1 < BASIS:
            taps = taps + rbase[1][4 * pair + 3 : 4 * pair + 4]
        taps = jnp.broadcast_to(taps, (ROWS, 128))
        shifted = bf16(pltpu.roll(taps, 0, 1, stride=1, stride_axis=0))
        rtable[:, pair * 128 : (pair + 1) * 128] = exact_dot(shifted, regroup)
    column_basis = iota((BASIS, DEPTH), 1) // 128 * 2 + iota((BASIS, DEPTH), 1) % 64 // 32
    widen = one_hot(iota((BASIS, DEPTH), 0) == column_basis)
    for visit in range(VISITS):
        for term in range(3):
            coefs[visit * 8 + term : visit * 8 + term + 1, 0:BASIS] = spatial[visit, term]
    plain = coefs[:, 0:BASIS]
    plain = jnp.where(iota(plain.shape, 0) % 8 < 3, plain, 0.0)
    top = bf16(plain)
    rest = plain - top.astype(jnp.float32)
    middle = bf16(rest)
    bottom = bf16(rest - middle.astype(jnp.float32))
    coefs[...] = exact_dot(top, widen) + exact_dot(middle, widen) + exact_dot(bottom, widen)
    first = (band * ROWS).astype(jnp.float32)
    u = (2.0 * (iota((ROWS, 1), 0).astype(jnp.float32) + first) + 1.0) / (bands * ROWS) - 1.0

    def fill_blend(visit, carry):
        coef = coefs[pl.ds(pl.multiple_of(visit * 8, 8), 8)]
        table = rtable[...]
        steady = table * (coef[0:1] + u * coef[1:2])
        slope = table * coef[2:3]
        full = jnp.concatenate([steady, slope], axis=0)
        high = bf16(full)
        low = bf16(full - high.astype(jnp.float32))
        blend[visit] = jnp.concatenate([high, low], axis=0)
        return carry

    lax.fori_loop(0, VISITS, fill_blend, 0)
    num[...] = jnp.zeros_like(num)
    den[...] = jnp.zeros_like(den)

    for d in range(1, 4):
        forward(d).wait_recv()

    def partner(i):
        half = (i + 1) // 2
        return n // 2 + half * (1 - 2 * (i % 2))

    side = me // 2 % 2
    owned = ((1 - core) * side + core * (2 + (side + height) % 2), 4 + side)

    def arrange(slot):
        turn_no = owned[slot]
        visit = 2 * (turn_no % 3) + height // 8
        table = keys[...].reshape(64, 128)
        patch_of = jnp.floor(table * (1.0 / 16.0))
        block_of = table - 16.0 * patch_of
        spread = one_hot(iota((128, 128), 0) == iota((128, 128), 1) % 16 + 16 * visit)
        source = iota((64, 128), 0) % 16 % 2 * 4 + iota((64, 128), 0) // 16
        held = source == iota((64, 128), 1) // 16
        gather = one_hot(iota((8, 64), 1) % 16 // 2 == iota((8, 64), 0))
        patch_of = jnp.where(held, exact_dot(bf16(patch_of), spread), 0.0)
        block_of = jnp.where(held, exact_dot(bf16(block_of), spread), 0.0)
        wanted = exact_dot(gather, bf16(patch_of)) * 16.0 + exact_dot(gather, bf16(block_of))
        wanted = wanted.astype(jnp.int32)
        pltpu.make_async_copy(y.at[slot], y.at[slot], r1.at[slot]).wait()
        data = y[slot].reshape(n * 16, 128)
        for part in range(4):
            place = iota((256, 128), 0) + 256 * part
            chosen = jnp.concatenate(
                [
                    one_hot(jnp.broadcast_to(wanted[k : k + 1], (256, 128)) == place)
                    for k in range(8)
                ],
                axis=1,
            )
            moved = exact_dot(chosen, data)
            z[slot, part * 16 : (part + 1) * 16] = bf16(moved.reshape(16, 2, 8, 128))

    def hand_out(slot):
        turn_no = owned[slot]

        def send_blocks(i, carry):
            peer = (me + partner(i)) % n
            pltpu.make_async_remote_copy(
                z.at[slot, peer],
                g.at[turn_no * 16 + height],
                s2.at[slot],
                r2.at[turn_no],
                device_id={"patch": peer},
                device_id_type=MESH,
            ).start()
            return carry

        lax.fori_loop(0, n - 1, send_blocks, 0)
        pltpu.make_async_copy(z.at[slot, me], g.at[turn_no * 16 + height], r2.at[turn_no]).start()

    arrange(0)

    @pl.when(owned[0] != 3)
    def _():
        hand_out(0)

    @pl.when(core == 0)
    def _():
        arrange(1)
        hand_out(1)

    def halo(turn_no, side):
        half, step = (1, 1) if side == 0 else (0, -1)
        return pltpu.make_async_remote_copy(
            g.at[pl.ds(turn_no * 16, 16), half],
            h.at[turn_no, side],
            sh.at[turn_no, side],
            rh.at[turn_no, side],
            device_id={"band": band + step},
            device_id_type=MESH,
        )

    w = (2.0 * iota((1, COLS), 1).astype(jnp.float32) + 1.0) / COLS - 1.0
    above_on = jnp.broadcast_to(band, (8, 128)) > 0
    below_on = jnp.broadcast_to(band, (8, 128)) < bands - 1
    left_lane = iota((128, 256), 1) % 128 < 64

    def filter_columns(turn_no, part):
        images = []
        for k in range(2):
            visit = 2 * turn_no + k
            if part == 0:
                blocks = [
                    g[visit * 8 + r, half].astype(jnp.float32) for r in range(8) for half in range(2)
                ]
            else:
                blocks = [
                    jnp.where(on, h[turn_no, place, k * 8 + r].astype(jnp.float32), 0.0)
                    for place, on in ((0, above_on), (1, below_on))
                    for r in range(8)
                ]
            images.append(bf16(jnp.concatenate(blocks, axis=0)))
        moved = exact_dot(order[part], jnp.concatenate(images, axis=1))
        beside = jnp.where(left_lane, moved[128:256], moved[256:384])
        window = jnp.concatenate(
            [
                jnp.concatenate([half[0:128, k * 128 : (k + 1) * 128] for half in (moved, beside)], 1)
                for k in range(2)
            ],
            axis=0,
        )
        window = bf16(window)
        for pair in range(PAIRS):
            result = bf16(exact_dot(window, ctable[:, pair * 256 : (pair + 1) * 256]))
            for k in range(2):
                for odd in range(2):
                    at = pair * 128 + part * 64 + odd * 32
                    for c in range(4):
                        filtered[turn_no, k, at : at + 32, c * 128 : (c + 1) * 128] = result[
                            k * 128 + c * 32 : k * 128 + (c + 1) * 32,
                            odd * 128 : (odd + 1) * 128,
                        ]

    def mix_rows(turn_no):
        for k in range(2):
            visit = 2 * turn_no + k
            mixed = exact_dot(blend[visit], filtered[turn_no, k])
            mixed = mixed[0:64] + mixed[64:128]
            matched[visit] = mixed[0:ROWS] + w * mixed[ROWS:64]

    def weigh_two(turn_no):
        pixels = []
        for k in range(2):
            unit = (VISITS + 2 * turn_no + k) * 8
            pixels.append(
                jnp.concatenate(
                    [g[unit + r, half].astype(jnp.float32) for r in range(8) for half in range(2)], 0
                )
            )
        turned = exact_dot(worder[...], bf16(jnp.concatenate(pixels, axis=1)))
        top, bottom = num[...], den[...]
        for k in range(2):
            weights = jnp.concatenate(
                [turned[c * ROWS : (c + 1) * ROWS, k * 128 : (k + 1) * 128] for c in range(4)], axis=1
            )
            top += weights * matched[2 * turn_no + k]
            bottom += weights
        num[...], den[...] = top, bottom

    def arrived(turn_no):
        part = g.at[pl.ds(turn_no * 16, 16)]
        pltpu.make_async_copy(part, part, r2.at[turn_no]).wait()

    def share_edges(turn_no):
        arrived(turn_no)

        @pl.when(band < bands - 1)
        def _():
            halo(turn_no, 0).start()

        @pl.when(band > 0)
        def _():
            halo(turn_no, 1).start()

    def filter_pair(i, carry):
        turn_no = (i + 2) % 3

        @pl.when(band < bands - 1)
        def _():
            halo(turn_no, 1).wait_recv()

        @pl.when(band > 0)
        def _():
            halo(turn_no, 0).wait_recv()

        filter_columns(turn_no, 1)
        mix_rows(turn_no)
        return carry

    def weigh_pair(i, carry):
        turn_no = (i + 1) % 3
        arrived(turn_no + 3)
        weigh_two(turn_no)
        return carry

    share_edges(2)

    @pl.when(owned[0] == 3)
    def _():
        hand_out(0)

    filter_columns(2, 0)
    def filter_inner(turn_no, carry):
        share_edges(turn_no)
        filter_columns(turn_no, 0)
        return carry

    lax.fori_loop(0, 2, filter_inner, 0)
    lax.fori_loop(0, 3, filter_pair, 0)
    lax.fori_loop(0, 3, weigh_pair, 0)
    o_ref[...] = num[...] / den[...]

    @pl.when(band < bands - 1)
    def _():
        for turn_no in range(3):
            halo(turn_no, 0).wait_send()

    @pl.when(band > 0)
    def _():
        for turn_no in range(3):
            halo(turn_no, 1).wait_send()

    told = keys.at[0, pl.ds(0, zs - 1)]
    pltpu.make_async_copy(told, told, sk).wait()
    for d in range(1, 4):
        forward(d).wait_send()
    for visit in range(VISITS):
        gone = rows.at[pl.ds(0, zs - 1)]
        pltpu.make_async_copy(gone, gone, s1.at[visit]).wait()

        @pl.when(lane4 != place_of(visit, height))
        def _():
            pltpu.make_async_copy(rows.at[0], rows.at[0], s1b.at[visit]).wait()

    relayed = z.at[0, pl.ds(0, n - 1)]
    pltpu.make_async_copy(relayed, relayed, s2.at[0]).wait()

    @pl.when(core == 0)
    def _():
        pltpu.make_async_copy(relayed, relayed, s2.at[1]).wait()


def orders():
    order = np.zeros((3, 4, 64, 256), np.float32)
    for c in range(4):
        for t in range(64):
            for kind, shift in ((0, 0), (1, 1), (2, -1)):
                d = c + shift
                if not 0 <= d < 4:
                    continue
                if t < 16:
                    place = (t % 8) * 8 + (t // 8) * 4 + d
                elif t < 48:
                    s = t - 16
                    place = 64 + (s % 8) * 16 + (s // 8) * 4 + d
                else:
                    s = t - 48
                    place = 192 + (s % 8) * 8 + (s // 8) * 4 + d
                order[kind, c, t, place] = 1.0
    worder = np.zeros((4, ROWS, 128), np.float32)
    for c in range(4):
        for s in range(ROWS):
            worder[c, s, (s % 8) * 16 + (s // 8) * 4 + c] = 1.0
    inner = order[:, :, 16:48, 64:192].reshape(384, 128)
    outer = np.concatenate([order[:, :, :16], order[:, :, 48:]], axis=2)
    outer = np.concatenate([outer[..., :64], outer[..., 192:]], axis=3).reshape(384, 128)
    return np.stack([inner, outer]), worder.reshape(128, 128)


def per_device(tile_flux, tile_weight, dest_patch, dest_block, basis, spatial):
    n = lax.axis_size("patch")
    vmem, dma = pltpu.VMEM, pltpu.SemaphoreType.DMA
    order, worder = orders()
    coadd = pl.pallas_call(
        kernel,
        out_shape=vmem((ROWS, COLS), jnp.float32),
        in_specs=[pl.BlockSpec(memory_space=pl.ANY)] * 8,
        out_specs=pl.BlockSpec(memory_space=vmem),
        scratch_shapes=[
            vmem((2, VISITS, 16, 8, 128), jnp.bfloat16),
            vmem((2, VISITS, 16), jnp.int32),
            vmem((BASIS, 2, TAPS), jnp.bfloat16),
            vmem((VISITS, 3, 1, BASIS), jnp.float32),
            vmem((48, 128), jnp.float32),
            vmem((2, 384, 128), jnp.bfloat16),
            vmem((128, 128), jnp.bfloat16),
            vmem((VISITS * 16, 16, 128), jnp.bfloat16),
            vmem((1, 128), jnp.float32),
            vmem((2, n, 16, 128), jnp.bfloat16),
            vmem((4, n // 4, 1, 128), jnp.float32),
            vmem((2, n, 2, 8, 128), jnp.bfloat16),
            vmem((VISITS * 16, 2, 8, 128), jnp.bfloat16),
            vmem((3, 2, 16, 8, 128), jnp.bfloat16),
            vmem((256, WIDE), jnp.bfloat16),
            vmem((ROWS, DEPTH), jnp.float32),
            vmem((VISITS * 8, DEPTH), jnp.float32),
            vmem((VISITS, 4 * ROWS, DEPTH), jnp.bfloat16),
            vmem((3, 2, DEPTH, COLS), jnp.bfloat16),
            vmem((VISITS, ROWS, COLS), jnp.float32),
            vmem((ROWS, COLS), jnp.float32),
            vmem((ROWS, COLS), jnp.float32),
            dma((8,)),
            pltpu.SemaphoreType.REGULAR((len(LEVELS),)),
            dma((VISITS,)),
            dma((VISITS,)),
            dma((2,)),
            dma,
            dma,
            dma((3,)),
            dma((3,)),
            dma((2,)),
            dma((VISITS,)),
            dma((3, 2)),
            dma((3, 2)),
        ],
        compiler_params=pltpu.CompilerParams(collective_id=0, has_side_effects=True),
        name="coadd",
    )(
        tile_flux,
        tile_weight,
        dest_patch,
        dest_block,
        basis.transpose(1, 0, 2),
        spatial.transpose(1, 2, 0, 3),
        jnp.asarray(order, jnp.bfloat16),
        jnp.asarray(worder, jnp.bfloat16),
    )
    return coadd[None]


def solution(mesh):
    in_specs = (
        P(None, ("patch", "band"), None, None),
        P(None, ("patch", "band"), None, None),
        P(None, ("patch", "band")),
        P(None, ("patch", "band")),
        P(),
        P("patch", None, None, None),
    )
    out_specs = P("patch", "band", None)
    return jax.shard_map(
        per_device, mesh=mesh, in_specs=in_specs, out_specs=out_specs, check_vma=False
    )
```
